128 devices in a mesh: ctx: 16 (over x, z_lo, core), heads: 8 (over z_hi, y).
Axes of the slice: x: 4, y: 4, z: 4 (z_hi: 2, z_lo: 2; z = z_hi * 2 + z_lo), core: 2. Of those that a mesh axis runs over, the one named last changes fastest.
Arguments:
- queries: bfloat16 [1024, 16384], P('ctx', 'heads'), may hold values from -40 to 40
- cache_keys: bfloat16 [2, 32768, 1024], P(None, 'ctx', 'heads'), may hold values from -10 to 10
- cache_values: bfloat16 [2, 32768, 1024], P(None, 'ctx', 'heads'), may hold values from -6 to 6
- bounds: int32 [2, 2], replicated, may hold values from 1 to 32768, as said below
- out_weight: bfloat16 [16384, 16384], P('heads', 'ctx'), may hold values from -0.046875 to 0.046875
- residual: bfloat16 [1024, 16384], P('heads', 'ctx'), may hold values from -3 to 3
Outputs:
- layer_out: bfloat16 [1024, 16384], P('heads', 'ctx')
The draws below stay inside these ranges and needn't reach their ends.
Inputs may be any that keep to these rules, and one draw needn't show every extreme that they name: bounds[p, 0] lies between 16384 and 32256; bounds[p, 1] - bounds[p, 0] lies between 1 and 512.
All inputs are finite; a program needn't handle non-finite values.
Results may differ from the reference program's by a relative error of at most 0.012.
Values may be sent and summed in bfloat16 or wider, within the bound.
A program may use at most 64 MiB of HBM per device.

```python
import math
import jax
import jax.numpy as jnp
from jax import lax

H = 128
KV = 8
HD = 128
D = 16384
PROMPTS = 2
Q = 512
CTX = 32768
ROWS = 1024


def shared_keys(key):
    base = jax.random.fold_in(key, 11)
    return 2.5 * jnp.clip(jax.random.normal(base, (PROMPTS, CTX, KV * HD), jnp.float32), -4.0, 4.0)


def draw_cache_keys(key, part):
    keys_all = shared_keys(key)
    return keys_all.astype(jnp.bfloat16)


def draw_queries(key, part):
    noise = jnp.clip(jax.random.normal(jax.random.fold_in(key, 23), (PROMPTS * Q, H * HD), jnp.float32), -4.0, 4.0)
    return noise.astype(jnp.bfloat16)


def draw_bounds(key, part):
    first_key, second_key, third_key = jax.random.split(jax.random.fold_in(key, 37), 3)
    start_first = CTX - Q - jax.random.randint(first_key, (1,), 0, Q)
    start_rest = jax.random.randint(second_key, (PROMPTS - 1,), CTX // 2, CTX - Q + 1)
    starts = jnp.concatenate([start_first, start_rest]).astype(jnp.int32)
    lengths = starts + jax.random.randint(third_key, (PROMPTS,), 1, Q + 1).astype(jnp.int32)
    return jnp.stack([starts, lengths], axis=1).astype(jnp.int32)


def levels(stream_key, shape, shards, least, high):
    def one(position, parts):
        steps = jax.random.uniform(jax.random.fold_in(jax.random.fold_in(stream_key, 6), position), (parts,), jnp.float32, least / len(shards), high / len(shards))
        return jnp.repeat(jnp.exp(steps), shape[position] // parts).reshape((-1,) + (1,) * (len(shape) - position - 1))

    level = one(*shards[0])
    for cut in shards[1:]:
        level = level * one(*cut)
    return level


def bell_draw(own_key, shape, spread, most, cuts=(), kind=jnp.bfloat16):
    values = spread * jax.random.normal(own_key, shape, jnp.float32)
    if cuts:
        values = values * levels(own_key, shape, cuts, -0.22, 0.18)
    return jnp.clip(values, -most, most).astype(kind)


def setup_inputs(seed: int = 0) -> dict:
    streams_of = jax.random.split(jax.random.key(seed), 7)
    return {
        "queries": draw_queries(jax.random.fold_in(streams_of[6], 71), 0),
        "cache_keys": draw_cache_keys(jax.random.fold_in(streams_of[6], 71), 0),
        "cache_values": bell_draw(streams_of[2], (PROMPTS, CTX, KV * HD), 1.0, 6.0, ((1, 16), (2, 8))),
        "bounds": draw_bounds(jax.random.fold_in(streams_of[6], 71), 0),
        "out_weight": bell_draw(streams_of[4], (D, D), D ** -0.5, 0.046875, ((0, 8), (1, 16))),
        "residual": bell_draw(streams_of[5], (ROWS, D), 0.5, 3.0, ((0, 8), (1, 16))),
    }


NEG_FILL = -1e+30

def reference(queries, cache_keys, cache_values, bounds, out_weight, residual):
    groups = H // KV
    scaling = 1.0 / math.sqrt(HD)
    key_pos = jnp.arange(CTX, dtype=jnp.int32)
    blocks = []
    for prompt in range(PROMPTS):
        begin = bounds[prompt, 0]
        length = bounds[prompt, 1]
        query_pos = begin + jnp.arange(Q, dtype=jnp.int32)
        visible = (key_pos[None, :] <= query_pos[:, None]) & (key_pos[None, :] < length)
        prompt_q = queries[prompt * Q:(prompt + 1) * Q].reshape(Q, H, HD)
        prompt_k = cache_keys[prompt].reshape(CTX, KV, HD)
        prompt_v = cache_values[prompt].reshape(CTX, KV, HD)

        def one_head(head):
            query_head = lax.dynamic_index_in_dim(prompt_q, head, 1, False)
            key_head = lax.dynamic_index_in_dim(prompt_k, head // groups, 1, False)
            value_head = lax.dynamic_index_in_dim(prompt_v, head // groups, 1, False)
            scores = jnp.dot(query_head, key_head.T, preferred_element_type=jnp.float32) * scaling
            scores = jnp.where(visible, scores, NEG_FILL)
            row_max = lax.optimization_barrier(jnp.max(scores, axis=1, keepdims=True))
            weights = jnp.where(visible, jnp.exp(scores - row_max), 0.0)
            total = lax.optimization_barrier(jnp.sum(weights, axis=1, keepdims=True))
            mixed = jnp.dot(weights.astype(jnp.bfloat16), value_head, preferred_element_type=jnp.float32)
            return (mixed / total).astype(jnp.bfloat16)
        heads_out = lax.map(one_head, jnp.arange(H, dtype=jnp.int32))
        blocks.append(jnp.transpose(heads_out, (1, 0, 2)).reshape(Q, H * HD))
    attended = jnp.concatenate(blocks, axis=0)
    projected = jnp.dot(attended, out_weight, preferred_element_type=jnp.float32)
    return (residual.astype(jnp.float32) + projected).astype(jnp.bfloat16)
```

```python
import functools
import math

import jax
import jax.numpy as jnp
from jax import lax
from jax.experimental import pallas as pl
from jax.experimental.pallas import tpu as pltpu
from jax.sharding import PartitionSpec as P

H = 128
KV = 8
HD = 128
Q = 512
GROUPS = H // KV
NEG = -1e30
LOG2E = 1.4426950408889634
SCALE2 = LOG2E / math.sqrt(HD)
CHIPS = 8
HALF = GROUPS // 2
BF16 = jnp.bfloat16
F32 = jnp.float32
MESH = pl.DeviceIdType.MESH


def chip_offset(k):
    return k // 2, (k + (k + 6) // 8) % 2


def kernel(
    bounds, q_ref, k_hbm, v_hbm, w_hbm, res_ref, out_ref,
    q_all, k_buf, v_buf, w_buf, s_a, s_b, m_a, m_b,
    o_all, lse_all, rc, rc_lse, mx, mx_lse, rx, rx_lse,
    att, pp, ry, zs, rz,
    local_sem, q_send, q_recv, qf_send,
    c_send, c_recv, cl_send, cl_recv,
    x_send, x_recv, xl_send, xl_recv,
    a_send, a_recv, af_send, y_send, y_recv, z_send, z_recv,
):
    me = lax.axis_index("ctx")
    hd = lax.axis_index("heads")
    x, zl, c = me // 4, (me // 2) % 2, me % 2
    zh, y = hd // 4, hd % 4
    rows = q_ref.shape[0]
    span = k_buf.shape[1]
    half_rows = HALF * rows

    def ctx_at(dx, dz, dc):
        return ((x + dx) % 4) * 4 + ((zl + dz) % 2) * 2 + (c + dc) % 2

    partner = ctx_at(0, 0, 1)

    def remote(src, dst, send, recv, **where):
        return pltpu.make_async_remote_copy(
            src_ref=src, dst_ref=dst, send_sem=send, recv_sem=recv,
            device_id=where, device_id_type=MESH,
        )

    load_k = pltpu.make_async_copy(k_hbm, k_buf, local_sem.at[0])
    load_v = pltpu.make_async_copy(v_hbm, v_buf.at[:, :, pl.ds(0, HD)], local_sem.at[1])
    load_w = pltpu.make_async_copy(w_hbm, w_buf, local_sem.at[2])
    load_k.start()
    load_v.start()
    load_w.start()

    barrier = pltpu.get_barrier_semaphore()
    pl.semaphore_signal(barrier, inc=1, device_id={"ctx": partner}, device_id_type=MESH)
    for k in range(1, CHIPS):
        dx, dz = chip_offset(k)
        pl.semaphore_signal(barrier, inc=1, device_id={"ctx": ctx_at(dx, dz, 0)}, device_id_type=MESH)
    for dy in range(1, 4):
        pl.semaphore_signal(barrier, inc=1, device_id={"heads": zh * 4 + (y + dy) % 4}, device_id_type=MESH)
    pl.semaphore_signal(barrier, inc=1, device_id={"heads": (1 - zh) * 4 + y}, device_id_type=MESH)
    q_all[0] = q_ref[...]
    for p in range(2):
        v_buf[p, :, pl.ds(HD, HD)] = jnp.ones((span, HD), BF16)
    pl.semaphore_wait(barrier, 1 + (CHIPS - 1) + 3 + 1)

    def q_own(k):
        dx, dz = chip_offset(k)
        return remote(q_ref, q_all.at[2 * k], q_send.at[k], q_recv.at[2 * k], ctx=ctx_at(-dx, -dz, 0))

    q_pair = remote(q_ref, q_all.at[1], q_send.at[0], q_recv.at[1], ctx=partner)
    q_pair.start()
    for k in range(1, CHIPS):
        q_own(k).start()

    def q_forward(k):
        return remote(q_all.at[2 * k], q_all.at[2 * k + 1], qf_send.at[k], q_recv.at[2 * k + 1], ctx=partner)

    load_k.wait()

    def place(n):
        k = n // 2
        dx, dz = chip_offset(k)
        t = ctx_at(dx, dz, n % 2)
        return t // 8, (t % 8) * rows

    def scores(n, half, s_ref, m_ref):
        p, within = place(n)
        block = jnp.concatenate(
            [q_all[n, :, pl.ds((half * HALF + j) * HD, HD)] for j in range(HALF)], axis=0
        )
        s = lax.dot_general(
            block, k_buf[p], (((1,), (1,)), ((), ())), preferred_element_type=F32
        )
        row = lax.broadcasted_iota(jnp.int32, (rows, 1), 0)
        limit = jnp.minimum(bounds[p, 0] + within + row, bounds[p, 1] - 1) - me * span
        limit = jnp.concatenate([limit] * HALF, axis=0)
        key = lax.broadcasted_iota(jnp.int32, (half_rows, span), 1)
        s = jnp.where(key <= limit, s, NEG)
        s_ref[...] = s
        m_ref[...] = jnp.broadcast_to(jnp.max(s, axis=1, keepdims=True), (half_rows, HD))

    def mix(n, half, s_ref, m_ref):
        p, _ = place(n)
        m = m_ref[...]
        weights = jnp.exp2((s_ref[...] - jnp.concatenate([m] * (span // HD), axis=1)) * SCALE2)
        both = jnp.dot(weights.astype(BF16), v_buf[p], preferred_element_type=F32)
        total = both[:, HD:]
        mixed = (both[:, :HD] / total).astype(BF16)
        lane = lax.broadcasted_iota(jnp.int32, (rows, HD), 1)
        m_c = jnp.zeros((rows, HD), F32)
        t_c = jnp.ones((rows, HD), F32)
        for j in range(HALF):
            h = half * HALF + j
            part = slice(j * rows, (j + 1) * rows)
            o_all[n, :, pl.ds(h * HD, HD)] = mixed[part]
            m_c = jnp.where(lane == h, m[part], m_c)
            t_c = jnp.where(lane == h, total[part], t_c)
        lse = m_c * SCALE2 + jnp.log(t_c) * LOG2E
        if half:
            lse = jnp.where(lane >= HALF, lse, lse_all[n])
        lse_all[n] = lse

    def merge(parts, out, out_lse):
        lses = [lse[...] for _, lse in parts]
        top = functools.reduce(jnp.maximum, lses)
        es = [jnp.exp2(lse - top) for lse in lses]
        tot = functools.reduce(lambda a, b: a + b, es)
        inv = 1.0 / tot
        if out_lse is not None:
            out_lse[...] = top + jnp.log(tot) * LOG2E
        ws = [e * inv for e in es]
        for h in range(GROUPS):
            cols = pl.ds(h * HD, HD)
            acc = None
            for (o, _), w in zip(parts, ws):
                term = o[:, cols].astype(F32) * jnp.broadcast_to(w[:, h:h + 1], (rows, HD))
                acc = term if acc is None else acc + term
            out[:, cols] = acc.astype(BF16)

    def pair_send(k):
        return (
            remote(o_all.at[2 * k + 1], rc.at[k], c_send.at[k], c_recv.at[k], ctx=partner),
            remote(lse_all.at[2 * k + 1], rc_lse.at[k], cl_send.at[k], cl_recv.at[k], ctx=partner),
        )

    def owner_send(k):
        dx, dz = chip_offset(k)
        to = ctx_at(dx, dz, 0)
        return (
            remote(mx.at[k], rx.at[k], x_send.at[k], x_recv.at[k], ctx=to),
            remote(mx_lse.at[k], rx_lse.at[k], xl_send.at[k], xl_recv.at[k], ctx=to),
        )

    def merge_pair(k):
        for copy in pair_send(k):
            copy.wait_recv()
        merge(
            [(o_all.at[2 * k], lse_all.at[2 * k]), (rc.at[k], rc_lse.at[k])],
            mx.at[k], mx_lse.at[k],
        )

    scores(0, 0, s_a, m_a)
    load_v.wait()
    steps = 2 * CHIPS

    def step(n, _):
        mix(n, 0, s_a, m_a)
        scores(n, 1, s_b, m_b)
        nxt = jnp.minimum(n + 1, steps - 1)

        @pl.when(n < steps - 1)
        def _():
            q_own_like(nxt).wait_recv()

        @pl.when((n % 2 == 1) & (n < steps - 1))
        def _():
            q_forward((n + 1) // 2).start()

        scores(nxt, 0, s_a, m_a)
        mix(n, 1, s_b, m_b)

        @pl.when(n % 2 == 1)
        def _():
            for copy in pair_send(n // 2):
                copy.start()

        @pl.when((n % 2 == 0) & (n >= 2))
        def _():
            k = n // 2 - 1
            merge_pair(k)

            @pl.when(k > 0)
            def _():
                for copy in owner_send(k):
                    copy.start()

        return 0

    def q_own_like(n):
        return remote(q_all.at[n], q_all.at[n], qf_send.at[0], q_recv.at[n], ctx=partner)

    lax.fori_loop(0, steps, step, 0)

    last = CHIPS - 1
    merge_pair(last)
    for copy in owner_send(last):
        copy.start()
    for k in range(1, CHIPS):
        for copy in owner_send(k):
            copy.wait_recv()
    merge(
        [(mx.at[0], mx_lse.at[0])] + [(rx.at[k], rx_lse.at[k]) for k in range(1, CHIPS)],
        att.at[0], None,
    )

    def a_own(k):
        dx, dz = chip_offset(k)
        return remote(att.at[0], att.at[2 * k], a_send.at[k], a_recv.at[2 * k], ctx=ctx_at(-dx, -dz, 0))

    def a_wait(n):
        return remote(att.at[n], att.at[n], af_send.at[0], a_recv.at[n], ctx=partner)

    def a_forward(k):
        return remote(att.at[2 * k], att.at[2 * k + 1], af_send.at[k], a_recv.at[2 * k + 1], ctx=partner)

    a_pair = remote(att.at[0], att.at[1], a_send.at[0], a_recv.at[1], ctx=partner)
    a_pair.start()
    for k in range(1, CHIPS):
        a_own(k).start()
    load_w.wait()

    def y_copy(k):
        dx, dz = chip_offset(k)
        hp = ((x + dx) % 4) * 2 + (zl + dz) % 2
        zp, yp = hp // 4, hp % 4
        return yp, zp, remote(pp.at[k], ry.at[zp, y], y_send.at[k], y_recv.at[zp, y], heads=zh * 4 + yp)

    def project(k, _):
        @pl.when(k < last)
        def _():
            a_wait(2 * k + 2).wait_recv()
            a_forward(k + 1).start()

        a_wait(2 * k + 1).wait_recv()
        both = jnp.concatenate([att[2 * k], att[2 * k + 1]], axis=0)
        done = jnp.dot(both, w_buf[...], preferred_element_type=F32).astype(BF16)
        pp[k, pl.ds(pl.multiple_of(c * rows, rows), rows), :] = done[:rows]
        pp[k, pl.ds(pl.multiple_of((1 - c) * rows, rows), rows), :] = done[rows:]
        yp, zp, copy = y_copy(k)

        @pl.when(yp != y)
        def _():
            copy.start()

        @pl.when(yp == y)
        def _():
            ry[zp, y] = pp[k]

        return 0

    lax.fori_loop(0, CHIPS, project, 0)

    def y_wait(zp, dy):
        ys = (y + dy) % 4
        return remote(ry.at[zp, ys], ry.at[zp, ys], y_send.at[0], y_recv.at[zp, ys], heads=zh * 4 + ys)

    far = 1 - zh
    for dy in range(1, 4):
        y_wait(far, dy).wait_recv()
    total = ry[far, 0].astype(F32)
    for ys in range(1, 4):
        total = total + ry[far, ys].astype(F32)
    zs[...] = total.astype(BF16)
    z_copy = remote(zs, rz, z_send, z_recv, heads=far * 4 + y)
    z_copy.start()
    for dy in range(1, 4):
        y_wait(zh, dy).wait_recv()
    total = res_ref[...].astype(F32)
    for ys in range(4):
        total = total + ry[zh, ys].astype(F32)
    z_copy.wait_recv()
    out_ref[...] = (total + rz[...].astype(F32)).astype(BF16)

    q_pair.wait_send()
    a_pair.wait_send()
    z_copy.wait_send()

    def drain(k, _):
        q_own(k).wait_send()
        q_forward(k).wait_send()
        a_own(k).wait_send()
        a_forward(k).wait_send()
        for copy in owner_send(k):
            copy.wait_send()
        return 0

    lax.fori_loop(1, CHIPS, drain, 0)

    def drain_all(k, _):
        for copy in pair_send(k):
            copy.wait_send()
        yp, _, copy = y_copy(k)

        @pl.when(yp != y)
        def _():
            copy.wait_send()

        return 0

    lax.fori_loop(0, CHIPS, drain_all, 0)


def shards(queries, cache_keys, cache_values, bounds, out_weight, residual):
    rows, cols = queries.shape
    prompts, span, hd = cache_keys.shape
    out_rows, width = residual.shape
    vmem = pl.BlockSpec(memory_space=pltpu.VMEM)
    hbm = pl.BlockSpec(memory_space=pl.ANY)
    n = 2 * CHIPS
    half_rows = HALF * rows
    dma = lambda *s: pltpu.SemaphoreType.DMA(s)
    return pl.pallas_call(
        kernel,
        out_shape=jax.ShapeDtypeStruct(residual.shape, BF16),
        in_specs=[pl.BlockSpec(memory_space=pltpu.SMEM), vmem, hbm, hbm, hbm, vmem],
        out_specs=vmem,
        scratch_shapes=[
            pltpu.VMEM((n, rows, cols), BF16),
            pltpu.VMEM((prompts, span, hd), BF16),
            pltpu.VMEM((prompts, span, 2 * hd), BF16),
            pltpu.VMEM(out_weight.shape, BF16),
            pltpu.VMEM((half_rows, span), F32),
            pltpu.VMEM((half_rows, span), F32),
            pltpu.VMEM((half_rows, hd), F32),
            pltpu.VMEM((half_rows, hd), F32),
            pltpu.VMEM((n, rows, cols), BF16),
            pltpu.VMEM((n, rows, hd), F32),
            pltpu.VMEM((CHIPS, rows, cols), BF16),
            pltpu.VMEM((CHIPS, rows, hd), F32),
            pltpu.VMEM((CHIPS, rows, cols), BF16),
            pltpu.VMEM((CHIPS, rows, hd), F32),
            pltpu.VMEM((CHIPS, rows, cols), BF16),
            pltpu.VMEM((CHIPS, rows, hd), F32),
            pltpu.VMEM((n, rows, cols), BF16),
            pltpu.VMEM((CHIPS, out_rows, width), BF16),
            pltpu.VMEM((2, 4, out_rows, width), BF16),
            pltpu.VMEM((out_rows, width), BF16),
            pltpu.VMEM((out_rows, width), BF16),
            dma(3), dma(CHIPS), dma(n), dma(CHIPS),
            dma(CHIPS), dma(CHIPS), dma(CHIPS), dma(CHIPS),
            dma(CHIPS), dma(CHIPS), dma(CHIPS), dma(CHIPS),
            dma(CHIPS), dma(n), dma(CHIPS), dma(CHIPS), dma(2, 4),
            pltpu.SemaphoreType.DMA, pltpu.SemaphoreType.DMA,
        ],
        compiler_params=pltpu.CompilerParams(
            collective_id=0, has_side_effects=True, vmem_limit_bytes=62 * 1024 * 1024
        ),
    )(bounds, queries, cache_keys, cache_values, out_weight, residual)


def solution(mesh):
    in_specs = (
        P("ctx", "heads"),
        P(None, "ctx", "heads"),
        P(None, "ctx", "heads"),
        P(),
        P("heads", "ctx"),
        P("heads", "ctx"),
    )
    out_specs = P("heads", "ctx")
    return jax.shard_map(shards, mesh=mesh, in_specs=in_specs, out_specs=out_specs, check_vma=False)
```

```python
import functools
import math

import jax
import jax.numpy as jnp
from jax import lax
from jax.experimental import pallas as pl
from jax.experimental.pallas import tpu as pltpu
from jax.sharding import PartitionSpec as P

H = 128
KV = 8
HD = 128
GROUPS = H // KV
NEG = -1e30
LOG2E = 1.4426950408889634
SCALE2 = LOG2E / math.sqrt(HD)
CHIPS = 8
SUBS = 2
LAST = SUBS * CHIPS - 1
BF16 = jnp.bfloat16
F32 = jnp.float32
MESH = pl.DeviceIdType.MESH
OFFSETS = ((0, 0), (0, 1), (1, 0), (3, 0), (2, 0), (2, 1), (1, 1), (3, 1))


def pick(k, values):
    if isinstance(k, int):
        return values[k]
    out = values[0]
    for j in range(1, len(values)):
        out = jnp.where(k == j, values[j], out)
    return out


def offset(k):
    return pick(k, [o[0] for o in OFFSETS]), pick(k, [o[1] for o in OFFSETS])


def sub_and_pair(m):
    rest = m - SUBS
    if isinstance(m, int):
        return (m, 0) if m < SUBS else (rest // (CHIPS - 1), rest % (CHIPS - 1) + 1)
    own = m < SUBS
    rest = jnp.maximum(rest, 0)
    return (
        jnp.where(own, m, rest // (CHIPS - 1)),
        jnp.where(own, 0, rest % (CHIPS - 1) + 1),
    )


def step_of(u, k):
    return u if k == 0 else SUBS + (CHIPS - 1) * u + k - 1


def kernel(
    bounds, q_ref, k_hbm, v_hbm, w_hbm, res_ref, out_ref,
    q_all, k_buf, v_buf, w_buf, s_a, s_b, m_a, m_b,
    o_all, lse_all, rc, rc_lse, mx, mx_lse, rx, rx_lse,
    att, pp, yl, yr, ra, rb, zs, rz,
    local_sem, *sems,
):
    q_sems, a_sems, (c_send, c_recv, cl_send, cl_recv), (x_send, x_recv, xl_send, xl_recv), (
        y1_send, y1_recv, y2_send, y2_recv, z_send, z_recv,
    ) = sems[:6], sems[6:12], sems[12:16], sems[16:20], sems[20:]
    me = lax.axis_index("ctx")
    hd = lax.axis_index("heads")
    x, zl, c = me // 4, (me // 2) % 2, me % 2
    zh, y = hd // 4, hd % 4
    hr = q_ref.shape[0] // SUBS
    hh = hr // 2
    span = k_buf.shape[1]
    unit = GROUPS * hr

    def ctx_at(dx, dz, dc):
        return ((x + dx) % 4) * 4 + ((zl + dz) % 2) * 2 + (c + dc) % 2

    partner = ctx_at(0, 0, 1)
    zpart = ctx_at(0, 1, 0)
    right = ctx_at(1, 0, 0)
    left = ctx_at(3, 0, 0)
    up = zh * 4 + (y + 1) % 4
    down = zh * 4 + (y + 3) % 4
    across = (1 - zh) * 4 + y

    def remote(src, dst, send, recv, **where):
        return pltpu.make_async_remote_copy(
            src_ref=src, dst_ref=dst, send_sem=send, recv_sem=recv,
            device_id=where, device_id_type=MESH,
        )

    load_k = pltpu.make_async_copy(k_hbm, k_buf, local_sem.at[0])
    load_v = pltpu.make_async_copy(v_hbm, v_buf.at[:, :, pl.ds(0, HD)], local_sem.at[1])
    load_w = pltpu.make_async_copy(w_hbm, w_buf, local_sem.at[2])
    load_k.start()
    load_v.start()
    load_w.start()

    barrier = pltpu.get_barrier_semaphore()
    pl.semaphore_signal(barrier, inc=1, device_id={"ctx": partner}, device_id_type=MESH)
    for k in range(1, CHIPS):
        dx, dz = offset(k)
        pl.semaphore_signal(barrier, inc=1, device_id={"ctx": ctx_at(dx, dz, 0)}, device_id_type=MESH)
    for to in (up, down, across):
        pl.semaphore_signal(barrier, inc=1, device_id={"heads": to}, device_id_type=MESH)
    for u in range(SUBS):
        q_all[u, 0, 0] = q_ref[pl.ds(u * hr, hr), :]
    for p in range(2):
        v_buf[p, :, pl.ds(HD, HD)] = jnp.ones((span, HD), BF16)
    pl.semaphore_wait(barrier, 1 + (CHIPS - 1) + 3)

    def gather(buf, sems, own):
        s0, sc, sz, sh, rv, rh = sems

        def whole(u, k, dc, send, to, src=None):
            return remote(buf.at[u, k, dc] if src is None else src, buf.at[u, k, dc], send, rv.at[u, k, dc], ctx=to)

        def part(u, k, top, src_k, send, to):
            i = 0 if top else 1
            rows = pl.ds(i * hh, hh)
            return remote(buf.at[u, src_k, 0, rows], buf.at[u, k, 0, rows], send, rh.at[u, k - 4, i], ctx=to)

        def stage(u, k):
            if k == 0:
                src = own(u)
                return [
                    whole(u, 0, 1, s0.at[u, 0], partner, src),
                    whole(u, 1, 0, s0.at[u, 1], zpart, src),
                    whole(u, 3, 0, s0.at[u, 2], right, src),
                    whole(u, 2, 0, s0.at[u, 3], left, src),
                ]
            here = buf.at[u, k, 0]
            out = []
            if k == 2:
                out.append(part(u, 4, False, 2, sh.at[u, 0], left))
                out.append(whole(u, 6, 0, sz.at[u, 0], zpart, here))
            if k == 3:
                out.append(part(u, 4, True, 3, sh.at[u, 1], right))
                out.append(whole(u, 7, 0, sz.at[u, 1], zpart, here))
            if k == 6:
                out.append(part(u, 5, False, 6, sh.at[u, 2], left))
            if k == 7:
                out.append(part(u, 5, True, 7, sh.at[u, 3], right))
            out.append(whole(u, k, 1, sc.at[u, k], partner, here))
            return out

        def arrive(u, k):
            if k in (4, 5):
                part(u, k, True, k, sh.at[u, 0], right).wait_recv()
                part(u, k, False, k, sh.at[u, 0], left).wait_recv()
            else:
                whole(u, k, 0, s0.at[u, 0], partner).wait_recv()

        def handle(u, k):
            if k:
                arrive(u, k)
            for copy in stage(u, k):
                copy.start()

        def wait_pair(u, k):
            whole(u, k, 1, s0.at[0, 0], partner).wait_recv()

        def drain(u):
            for k in range(CHIPS):
                for copy in stage(u, k):
                    copy.wait_send()

        return handle, wait_pair, drain, stage

    q_handle, q_wait_pair, q_drain, q_stage = gather(q_all, q_sems, lambda u: q_ref.at[pl.ds(u * hr, hr)])
    a_handle, a_wait_pair, a_drain, _ = gather(att, a_sems, lambda u: att.at[u, 0, 0])

    q_handle(0, 0)
    for u in range(1, SUBS):
        q_stage(u, 0)[0].start()

    def q_rest(u):
        for copy in q_stage(u, 0)[1:]:
            copy.start()

    load_k.wait()

    def place(m, dc):
        u, k = sub_and_pair(m)
        dx, dz = offset(k)
        t = ctx_at(dx, dz, dc)
        return t // 8, (t % 8) * (hr * SUBS) + u * hr

    def scores(m, dc, s_ref, m_ref):
        u, k = sub_and_pair(m)
        p, within = place(m, dc)
        block = jnp.concatenate(
            [q_all[u, k, dc, :, pl.ds(j * HD, HD)] for j in range(GROUPS)], axis=0
        )
        s = lax.dot_general(
            block, k_buf[p], (((1,), (1,)), ((), ())), preferred_element_type=F32
        )
        row = lax.broadcasted_iota(jnp.int32, (hr, 1), 0)
        limit = jnp.minimum(bounds[p, 0] + within + row, bounds[p, 1] - 1) - me * span
        limit = jnp.concatenate([limit] * GROUPS, axis=0)
        key = lax.broadcasted_iota(jnp.int32, (unit, span), 1)
        s = jnp.where(key <= limit, s, NEG)
        s_ref[...] = s
        m_ref[...] = jnp.broadcast_to(jnp.max(s, axis=1, keepdims=True), (unit, HD))

    def mix(m, dc, s_ref, m_ref):
        p, _ = place(m, dc)
        top = m_ref[...]
        weights = jnp.exp2((s_ref[...] - jnp.concatenate([top] * (span // HD), axis=1)) * SCALE2)
        both = jnp.dot(weights.astype(BF16), v_buf[p], preferred_element_type=F32)
        total = both[:, HD:]
        mixed = (both[:, :HD] / total).astype(BF16)
        lane = lax.broadcasted_iota(jnp.int32, (hr, HD), 1)
        m_c = jnp.zeros((hr, HD), F32)
        t_c = jnp.ones((hr, HD), F32)
        for h in range(GROUPS):
            part = slice(h * hr, (h + 1) * hr)
            o_all[m, dc, :, pl.ds(h * HD, HD)] = mixed[part]
            m_c = jnp.where(lane == h, top[part], m_c)
            t_c = jnp.where(lane == h, total[part], t_c)
        lse_all[m, dc] = m_c * SCALE2 + jnp.log(t_c) * LOG2E

    def merge(parts, out, out_lse):
        lses = [lse[...] for _, lse in parts]
        top = functools.reduce(jnp.maximum, lses)
        es = [jnp.exp2(lse - top) for lse in lses]
        tot = functools.reduce(lambda a, b: a + b, es)
        inv = 1.0 / tot
        if out_lse is not None:
            out_lse[...] = top + jnp.log(tot) * LOG2E
        ws = [e * inv for e in es]
        for h in range(GROUPS):
            cols = pl.ds(h * HD, HD)
            acc = None
            for (o, _), w in zip(parts, ws):
                term = o[:, cols].astype(F32) * jnp.broadcast_to(w[:, h:h + 1], (hr, HD))
                acc = term if acc is None else acc + term
            out[:, cols] = acc.astype(BF16)

    def pair_send(m):
        return (
            remote(o_all.at[m, 1], rc.at[m], c_send.at[m], c_recv.at[m], ctx=partner),
            remote(lse_all.at[m, 1], rc_lse.at[m], cl_send.at[m], cl_recv.at[m], ctx=partner),
        )

    def owner_send(m):
        _, k = sub_and_pair(m)
        dx, dz = offset(k)
        to = ctx_at(dx, dz, 0)
        return (
            remote(mx.at[m], rx.at[m], x_send.at[m], x_recv.at[m], ctx=to),
            remote(mx_lse.at[m], rx_lse.at[m], xl_send.at[m], xl_recv.at[m], ctx=to),
        )

    def start_pair(m):
        for copy in pair_send(m):
            copy.start()

    def merge_pair(m):
        for copy in pair_send(m):
            copy.wait_recv()
        merge(
            [(o_all.at[m, 0], lse_all.at[m, 0]), (rc.at[m], rc_lse.at[m])],
            mx.at[m], mx_lse.at[m],
        )

    def start_owner(m):
        for copy in owner_send(m):
            copy.start()

    def finish(u):
        for k in range(1, CHIPS):
            for copy in owner_send(step_of(u, k)):
                copy.wait_recv()
        merge(
            [(mx.at[step_of(u, 0)], mx_lse.at[step_of(u, 0)])]
            + [(rx.at[step_of(u, k)], rx_lse.at[step_of(u, k)]) for k in range(1, CHIPS)],
            att.at[u, 0, 0], None,
        )
        a_handle(u, 0)

    def project(u, ks):
        block = jnp.concatenate([att[u, k, dc] for k in ks for dc in range(2)], axis=0)
        done = jnp.dot(block, w_buf[...], preferred_element_type=F32).astype(BF16)
        i = 0
        for k in ks:
            dx, dz = offset(k)
            hp = ((x + dx) % 4) * 2 + (zl + dz) % 2
            for dc in range(2):
                pp[u, hp // 4, hp % 4, (c + dc) % 2] = done[i * hr:(i + 1) * hr]
                i += 1

    def y1_copies(u, zp):
        yy = (y + 2) % 4
        return (
            remote(pp.at[u, zp, yy, 0], yl.at[u, zp], y1_send.at[u, zp, 0], y1_recv.at[u, zp, 0], heads=up),
            remote(pp.at[u, zp, yy, 1], yr.at[u, zp], y1_send.at[u, zp, 1], y1_recv.at[u, zp, 1], heads=down),
        )

    def y2_copies(u, zp):
        return (
            remote(pp.at[u, zp, (y + 1) % 4], ra.at[u, zp], y2_send.at[u, zp, 0], y2_recv.at[u, zp, 0], heads=up),
            remote(pp.at[u, zp, (y + 3) % 4], rb.at[u, zp], y2_send.at[u, zp, 1], y2_recv.at[u, zp, 1], heads=down),
        )

    far = 1 - zh

    def y_first(u):
        for zp in (far, zh):
            for copy in y1_copies(u, zp):
                copy.start()

    def y_second(u):
        for zp in (far, zh):
            for i, (first, second) in enumerate(zip(y1_copies(u, zp), y2_copies(u, zp))):
                first.wait_recv()
                yy = (y + 1 + 2 * i) % 4
                got = (yl, yr)[i]
                pp[u, zp, yy, i] = (pp[u, zp, yy, i].astype(F32) + got[u, zp].astype(F32)).astype(BF16)
                second.start()

    def z_copy(u):
        return remote(zs.at[u], rz.at[u], z_send.at[u], z_recv.at[u], heads=across)

    def y_total(u, zp):
        for copy in y2_copies(u, zp):
            copy.wait_recv()
        return pp[u, zp, y].astype(F32) + ra[u, zp].astype(F32) + rb[u, zp].astype(F32)

    def z_start(u):
        zs[u] = y_total(u, far).astype(BF16)
        z_copy(u).start()

    def emit(u):
        total = y_total(u, zh)
        z_copy(u).wait_recv()
        total = total + rz[u].astype(F32)
        for cc in range(2):
            rows = pl.ds(cc * hr * SUBS + u * hr, hr)
            out_ref[rows, :] = (res_ref[rows, :].astype(F32) + total[cc]).astype(BF16)

    scores(0, 0, s_a, m_a)
    load_v.wait()

    events = {
        1: [lambda: q_handle(0, 1), lambda: q_handle(0, 2), lambda: q_handle(0, 3)],
        3: [lambda: q_handle(0, 4), lambda: q_rest(1)],
        4: [lambda: q_handle(0, 6), lambda: q_handle(0, 7)],
        5: [lambda: q_handle(0, 5)],
        6: [lambda: q_handle(1, 1), lambda: q_handle(1, 2), lambda: q_handle(1, 3)],
        8: [lambda: q_handle(1, 4)],
        9: [lambda: q_handle(1, 6), lambda: q_handle(1, 7)],
        11: [lambda: q_handle(1, 5)],
        12: [lambda: finish(0)],
        14: [lambda: a_handle(0, 1), lambda: a_handle(0, 2), lambda: a_handle(0, 3)],
        15: [lambda: a_handle(0, 4)],
    }

    def step(m, _):
        for at, acts in events.items():
            @pl.when(m == at)
            def _():
                for act in acts:
                    act()

        u, k = sub_and_pair(m)
        q_wait_pair(u, k)

        @pl.when(m >= 1)
        def _():
            start_pair(m - 1)

        @pl.when(m >= 2)
        def _():
            merge_pair(m - 2)

            @pl.when(m - 2 >= SUBS)
            def _():
                start_owner(m - 2)

        nxt = jnp.minimum(m + 1, LAST)
        scores(m, 1, s_b, m_b)
        mix(m, 0, s_a, m_a)
        scores(nxt, 0, s_a, m_a)
        mix(m, 1, s_b, m_b)
        return 0

    lax.fori_loop(0, LAST + 1, step, 0)

    start_pair(LAST)
    merge_pair(LAST - 1)
    start_owner(LAST - 1)
    merge_pair(LAST)
    start_owner(LAST)

    load_w.wait()
    early, late = (0, 1, 2, 3), (4, 5, 6, 7)

    def pairs_in(u, ks):
        for k in ks:
            a_wait_pair(u, k)

    a_handle(0, 6)
    a_handle(0, 7)
    pairs_in(0, early)
    project(0, early)
    a_handle(0, 5)
    finish(1)
    pairs_in(0, late)
    project(0, late)
    y_first(0)
    a_handle(1, 1)
    a_handle(1, 2)
    a_handle(1, 3)
    y_second(0)
    pairs_in(1, early)
    project(1, early)
    a_handle(1, 4)
    z_start(0)
    a_handle(1, 6)
    a_handle(1, 7)
    emit(0)
    a_handle(1, 5)
    pairs_in(1, late)
    project(1, late)
    y_first(1)
    y_second(1)
    z_start(1)
    emit(1)

    for u in range(SUBS):
        q_drain(u)
        a_drain(u)
        z_copy(u).wait_send()
        for zp in range(2):
            for copy in y1_copies(u, zp) + y2_copies(u, zp):
                copy.wait_send()

    def drain(m, _):
        for copy in pair_send(m):
            copy.wait_send()

        @pl.when(m >= SUBS)
        def _():
            for copy in owner_send(m):
                copy.wait_send()

        return 0

    lax.fori_loop(0, LAST + 1, drain, 0)


def shards(queries, cache_keys, cache_values, bounds, out_weight, residual):
    rows, cols = queries.shape
    prompts, span, hd = cache_keys.shape
    out_rows, width = residual.shape
    hr = rows // SUBS
    vmem = pl.BlockSpec(memory_space=pltpu.VMEM)
    hbm = pl.BlockSpec(memory_space=pl.ANY)
    n = SUBS * CHIPS
    unit = GROUPS * hr
    dma = lambda *s: pltpu.SemaphoreType.DMA(s)
    gather_sems = [
        dma(SUBS, 4), dma(SUBS, CHIPS), dma(SUBS, 2), dma(SUBS, 4), dma(SUBS, CHIPS, 2), dma(SUBS, 2, 2),
    ]
    return pl.pallas_call(
        kernel,
        out_shape=jax.ShapeDtypeStruct(residual.shape, BF16),
        in_specs=[pl.BlockSpec(memory_space=pltpu.SMEM), vmem, hbm, hbm, hbm, vmem],
        out_specs=vmem,
        scratch_shapes=[
            pltpu.VMEM((SUBS, CHIPS, 2, hr, cols), BF16),
            pltpu.VMEM((prompts, span, hd), BF16),
            pltpu.VMEM((prompts, span, 2 * hd), BF16),
            pltpu.VMEM(out_weight.shape, BF16),
            pltpu.VMEM((unit, span), F32),
            pltpu.VMEM((unit, span), F32),
            pltpu.VMEM((unit, hd), F32),
            pltpu.VMEM((unit, hd), F32),
            pltpu.VMEM((n, 2, hr, cols), BF16),
            pltpu.VMEM((n, 2, hr, hd), F32),
            pltpu.VMEM((n, hr, cols), BF16),
            pltpu.VMEM((n, hr, hd), F32),
            pltpu.VMEM((n, hr, cols), BF16),
            pltpu.VMEM((n, hr, hd), F32),
            pltpu.VMEM((n, hr, cols), BF16),
            pltpu.VMEM((n, hr, hd), F32),
            pltpu.VMEM((SUBS, CHIPS, 2, hr, cols), BF16),
            pltpu.VMEM((SUBS, 2, 4, 2, hr, width), BF16),
            pltpu.VMEM((SUBS, 2, hr, width), BF16),
            pltpu.VMEM((SUBS, 2, hr, width), BF16),
            pltpu.VMEM((SUBS, 2, 2, hr, width), BF16),
            pltpu.VMEM((SUBS, 2, 2, hr, width), BF16),
            pltpu.VMEM((SUBS, 2, hr, width), BF16),
            pltpu.VMEM((SUBS, 2, hr, width), BF16),
            dma(3), *gather_sems, *gather_sems,
            dma(n), dma(n), dma(n), dma(n),
            dma(n), dma(n), dma(n), dma(n),
            dma(SUBS, 2, 2), dma(SUBS, 2, 2), dma(SUBS, 2, 2), dma(SUBS, 2, 2), dma(SUBS), dma(SUBS),
        ],
        compiler_params=pltpu.CompilerParams(
            collective_id=0, has_side_effects=True, vmem_limit_bytes=62 * 1024 * 1024
        ),
    )(bounds, queries, cache_keys, cache_values, out_weight, residual)


def solution(mesh):
    in_specs = (
        P("ctx", "heads"),
        P(None, "ctx", "heads"),
        P(None, "ctx", "heads"),
        P(),
        P("heads", "ctx"),
        P("heads", "ctx"),
    )
    out_specs = P("heads", "ctx")
    return jax.shard_map(shards, mesh=mesh, in_specs=in_specs, out_specs=out_specs, check_vma=False)
```

```python
import functools
import math

import jax
import jax.numpy as jnp
from jax import lax
from jax.experimental import pallas as pl
from jax.experimental.pallas import tpu as pltpu
from jax.sharding import PartitionSpec as P

H = 128
KV = 8
HD = 128
GROUPS = H // KV
NEG = -1e30
LOG2E = 1.4426950408889634
SCALE2 = LOG2E / math.sqrt(HD)
CHIPS = 8
SUBS = 2
LAST = SUBS * CHIPS - 1
BF16 = jnp.bfloat16
F32 = jnp.float32
MESH = pl.DeviceIdType.MESH
OFFSETS = ((0, 0), (0, 1), (1, 0), (3, 0), (2, 0), (2, 1), (1, 1), (3, 1))
STEPS = tuple(
    [(0, 0), (1, 0)]
    + [(0, k) for k in (1, 2, 3, 4, 5, 6, 7)]
    + [(1, k) for k in (4, 6, 5, 7, 1, 2, 3)]
)


def pick(k, values):
    if isinstance(k, int):
        return values[k]
    out = values[0]
    for j in range(1, len(values)):
        out = jnp.where(k == j, values[j], out)
    return out


def offset(k):
    return pick(k, [o[0] for o in OFFSETS]), pick(k, [o[1] for o in OFFSETS])


def sub_and_pair(m):
    return pick(m, [u for u, _ in STEPS]), pick(m, [k for _, k in STEPS])


def step_of(u, k):
    return STEPS.index((u, k))


def unit_of(m, i):
    if isinstance(m, int) and m < SUBS:
        return i, 0, m
    return *sub_and_pair(m), i


def slot_of(m, i):
    return (i, m) if isinstance(m, int) and m < SUBS else (m, i)


def kernel(
    bounds, q_ref, k_hbm, v_hbm, w_hbm, res_ref, out_ref,
    q_all, k_buf, v_buf, w_buf, s_a, s_b, m_a, m_b,
    o_all, lse_all, rc, rc_lse, mx, mx_lse, rx, rx_lse, xr, xr_lse,
    att, pp, yl, yr, ra, rb, zs, zr, rz,
    local_sem, *sems,
):
    q_sems, a_sems, (c_send, c_recv, cl_send, cl_recv), (x_send, x_recv, xl_send, xl_recv), (
        y1_send, y1_recv, y2_send, y2_recv, z1_send, z1_recv, z2_send, z2_recv,
        h1_send, h1_recv, h2_send, h2_recv,
    ) = sems[:5], sems[5:10], sems[10:14], sems[14:18], sems[18:]
    me = lax.axis_index("ctx")
    hd = lax.axis_index("heads")
    x, zl, c = me // 4, (me // 2) % 2, me % 2
    zh, y = hd // 4, hd % 4
    hr = q_ref.shape[0] // SUBS
    hh = hr // 2
    span = k_buf.shape[1]
    unit = GROUPS * hr

    def ctx_at(dx, dz, dc):
        return ((x + dx) % 4) * 4 + ((zl + dz) % 2) * 2 + (c + dc) % 2

    partner = ctx_at(0, 0, 1)
    zpart = ctx_at(0, 1, 0)
    right = ctx_at(1, 0, 0)
    left = ctx_at(3, 0, 0)
    up = zh * 4 + (y + 1) % 4
    down = zh * 4 + (y + 3) % 4
    above = ((zh + zl) % 2) * 4 + y
    below = ((zh + 1 - zl) % 2) * 4 + y
    other = (1 - zh) * 4 + y

    def remote(src, dst, send, recv, **where):
        return pltpu.make_async_remote_copy(
            src_ref=src, dst_ref=dst, send_sem=send, recv_sem=recv,
            device_id=where, device_id_type=MESH,
        )

    load_k = pltpu.make_async_copy(k_hbm, k_buf, local_sem.at[0])
    load_v = pltpu.make_async_copy(v_hbm, v_buf.at[:, :, pl.ds(0, HD)], local_sem.at[1])
    load_w = pltpu.make_async_copy(w_hbm, w_buf, local_sem.at[2])
    load_k.start()
    load_v.start()
    load_w.start()

    barrier = pltpu.get_barrier_semaphore()
    pl.semaphore_signal(barrier, inc=1, device_id={"ctx": partner}, device_id_type=MESH)
    for k in range(1, CHIPS):
        dx, dz = offset(k)
        pl.semaphore_signal(barrier, inc=1, device_id={"ctx": ctx_at(dx, dz, 0)}, device_id_type=MESH)
    for to in (up, down):
        pl.semaphore_signal(barrier, inc=1, device_id={"heads": to}, device_id_type=MESH)
    pl.semaphore_signal(barrier, inc=1, device_id={"ctx": zpart, "heads": other}, device_id_type=MESH)
    for u in range(SUBS):
        q_all[u, 0, 0] = q_ref[pl.ds(u * hr, hr), :]
    for p in range(2):
        v_buf[p, :, pl.ds(HD, HD)] = jnp.ones((span, HD), BF16)

    def gather(buf, sems, own):
        s0, sc, sh, rv, rh = sems

        def whole(u, k, dc, send, to, src=None):
            return remote(buf.at[u, k, dc] if src is None else src, buf.at[u, k, dc], send, rv.at[u, k, dc], ctx=to)

        def part(u, k, top, src_k, send, to):
            i = 0 if top else 1
            rows = pl.ds(i * hh, hh)
            return remote(buf.at[u, src_k, 0, rows], buf.at[u, k, 0, rows], send, rh.at[u, k - 4, i], ctx=to)

        top, bottom = True, False

        def stage(u, k):
            if k == 0:
                src = own(u)
                return [
                    whole(u, 0, 1, s0.at[u, 0], partner, src),
                    whole(u, 1, 0, s0.at[u, 1], zpart, src),
                    whole(u, 3, 0, s0.at[u, 2], right, src),
                    whole(u, 2, 0, s0.at[u, 3], left, src),
                ]
            here = buf.at[u, k, 0]
            out = []
            if k == 1:
                out.append(part(u, 7, bottom, 1, sh.at[u, 4], right))
                out.append(part(u, 6, bottom, 1, sh.at[u, 5], left))
            if k == 2:
                out.append(part(u, 6, top, 2, sh.at[u, 6], zpart))
                out.append(part(u, 4, bottom, 2, sh.at[u, 0], left))
            if k == 3:
                out.append(part(u, 7, top, 3, sh.at[u, 7], zpart))
                out.append(part(u, 4, top, 3, sh.at[u, 1], right))
            if k == 6:
                out.append(part(u, 5, bottom, 6, sh.at[u, 2], left))
            if k == 7:
                out.append(part(u, 5, top, 7, sh.at[u, 3], right))
            out.append(whole(u, k, 1, sc.at[u, k], partner, here))
            return out

        def arrive(u, k):
            if k >= 4:
                part(u, k, True, k, sh.at[u, 0], right).wait_recv()
                part(u, k, False, k, sh.at[u, 0], left).wait_recv()
            else:
                whole(u, k, 0, s0.at[u, 0], partner).wait_recv()

        def handle(u, k):
            if k:
                arrive(u, k)
            for copy in stage(u, k):
                copy.start()

        def wait_pair(u, k):
            whole(u, k, 1, s0.at[0, 0], partner).wait_recv()

        def drain(u):
            for k in range(CHIPS):
                for copy in stage(u, k):
                    copy.wait_send()

        return handle, wait_pair, drain, stage

    q_handle, q_wait_pair, q_drain, q_stage = gather(q_all, q_sems, lambda u: q_ref.at[pl.ds(u * hr, hr)])
    a_handle, a_wait_pair, a_drain, _ = gather(att, a_sems, lambda u: att.at[u, 0, 0])

    def q_rest(u):
        for copy in q_stage(u, 0)[1:]:
            copy.start()

    def place(u, k, dc):
        dx, dz = offset(k)
        t = ctx_at(dx, dz, dc)
        return t // 8, (t % 8) * (hr * SUBS) + u * hr

    def scores(m, i, s_ref, m_ref):
        u, k, dc = unit_of(m, i)
        p, within = place(u, k, dc)
        block = jnp.concatenate(
            [q_all[u, k, dc, :, pl.ds(j * HD, HD)] for j in range(GROUPS)], axis=0
        )
        s = lax.dot_general(
            block, k_buf[p], (((1,), (1,)), ((), ())), preferred_element_type=F32
        )
        row = lax.broadcasted_iota(jnp.int32, (hr, 1), 0)
        limit = jnp.minimum(bounds[p, 0] + within + row, bounds[p, 1] - 1) - me * span
        limit = jnp.concatenate([limit] * GROUPS, axis=0)
        key = lax.broadcasted_iota(jnp.int32, (unit, span), 1)
        s = jnp.where(key <= limit, s, NEG)
        s_ref[...] = s
        m_ref[...] = jnp.broadcast_to(jnp.max(s, axis=1, keepdims=True), (unit, HD))

    def mix(m, i, s_ref, m_ref):
        u, k, dc = unit_of(m, i)
        p, _ = place(u, k, dc)
        to, core = slot_of(m, i)
        top = m_ref[...]
        weights = jnp.exp2((s_ref[...] - jnp.concatenate([top] * (span // HD), axis=1)) * SCALE2)
        both = jnp.dot(weights.astype(BF16), v_buf[p], preferred_element_type=F32)
        total = both[:, HD:]
        mixed = (both[:, :HD] / total).astype(BF16)
        lane = lax.broadcasted_iota(jnp.int32, (hr, HD), 1)
        m_c = jnp.zeros((hr, HD), F32)
        t_c = jnp.ones((hr, HD), F32)
        for h in range(GROUPS):
            part = slice(h * hr, (h + 1) * hr)
            o_all[to, core, :, pl.ds(h * HD, HD)] = mixed[part]
            m_c = jnp.where(lane == h, top[part], m_c)
            t_c = jnp.where(lane == h, total[part], t_c)
        lse_all[to, core] = m_c * SCALE2 + jnp.log(t_c) * LOG2E

    def merge(parts, out, out_lse):
        lses = [lse[...] for _, lse in parts]
        top = functools.reduce(jnp.maximum, lses)
        es = [jnp.exp2(lse - top) for lse in lses]
        tot = functools.reduce(lambda a, b: a + b, es)
        inv = 1.0 / tot
        if out_lse is not None:
            out_lse[...] = top + jnp.log(tot) * LOG2E
        ws = [e * inv for e in es]
        for h in range(GROUPS):
            cols = pl.ds(h * HD, HD)
            acc = None
            for (o, _), w in zip(parts, ws):
                term = o[:, cols].astype(F32) * jnp.broadcast_to(w[:, h:h + 1], (hr, HD))
                acc = term if acc is None else acc + term
            out[:, cols] = acc.astype(BF16)

    def pair_send(m):
        return (
            remote(o_all.at[m, 1], rc.at[m], c_send.at[m], c_recv.at[m], ctx=partner),
            remote(lse_all.at[m, 1], rc_lse.at[m], cl_send.at[m], cl_recv.at[m], ctx=partner),
        )

    def owner_send(m):
        _, k = sub_and_pair(m)
        dx, dz = offset(k)
        to = ctx_at(dx, dz, 0)
        return (
            remote(mx.at[m], rx.at[m], x_send.at[m], x_recv.at[m], ctx=to),
            remote(mx_lse.at[m], rx_lse.at[m], xl_send.at[m], xl_recv.at[m], ctx=to),
        )

    def half_copies(u, k, forward):
        m, d, dz = step_of(u, k), 2 * u + k - 4, OFFSETS[k][1]
        out = []
        for i in range(2):
            rows = pl.ds(i * hh, hh)
            if forward:
                to = ctx_at((1, 3)[i], dz, 0)
                out.append(remote(xr.at[d, rows], rx.at[m, rows], h2_send.at[d, i, 0], h2_recv.at[d, i, 0], ctx=to))
                out.append(remote(xr_lse.at[d, rows], rx_lse.at[m, rows], h2_send.at[d, i, 1], h2_recv.at[d, i, 1], ctx=to))
            else:
                to = (right, left)[i]
                out.append(remote(mx.at[m, rows], xr.at[d, rows], h1_send.at[d, i, 0], h1_recv.at[d, i, 0], ctx=to))
                out.append(remote(mx_lse.at[m, rows], xr_lse.at[d, rows], h1_send.at[d, i, 1], h1_recv.at[d, i, 1], ctx=to))
        return out

    def half_start(u, k):
        for copy in half_copies(u, k, False):
            copy.start()

    def half_forward(u, k):
        for copy in half_copies(u, k, False):
            copy.wait_recv()
        for copy in half_copies(u, k, True):
            copy.start()

    def start_pair(m):
        for copy in pair_send(m):
            copy.start()

    def merge_pair(m):
        for copy in pair_send(m):
            copy.wait_recv()
        merge(
            [(o_all.at[m, 0], lse_all.at[m, 0]), (rc.at[m], rc_lse.at[m])],
            mx.at[m], mx_lse.at[m],
        )

    def start_owner(m):
        for copy in owner_send(m):
            copy.start()

    def finish(u):
        for copy in pair_send(u):
            copy.wait_recv()
        for k in range(1, CHIPS):
            for copy in half_copies(u, k, True) if k in (4, 5) else owner_send(step_of(u, k)):
                copy.wait_recv()
        merge(
            [(o_all.at[u, 0], lse_all.at[u, 0]), (rc.at[u], rc_lse.at[u])]
            + [(rx.at[step_of(u, k)], rx_lse.at[step_of(u, k)]) for k in range(1, CHIPS)],
            att.at[u, 0, 0], None,
        )
        a_handle(u, 0)

    def project(u, ks):
        block = jnp.concatenate([att[u, k, dc] for k in ks for dc in range(2)], axis=0)
        done = jnp.dot(block, w_buf[...], preferred_element_type=F32).astype(BF16)
        i = 0
        for k in ks:
            dx, dz = offset(k)
            hp = ((x + dx) % 4) * 2 + (zl + dz) % 2
            for dc in range(2):
                pp[u, hp // 4, hp % 4, (c + dc) % 2] = done[i * hr:(i + 1) * hr]
                i += 1

    def y1_copies(u, zp):
        yy = (y + 2) % 4
        return (
            remote(pp.at[u, zp, yy, 0], yl.at[u, zp], y1_send.at[u, zp, 0], y1_recv.at[u, zp, 0], heads=up),
            remote(pp.at[u, zp, yy, 1], yr.at[u, zp], y1_send.at[u, zp, 1], y1_recv.at[u, zp, 1], heads=down),
        )

    def y2_copies(u, zp):
        return (
            remote(pp.at[u, zp, (y + 1) % 4], ra.at[u, zp], y2_send.at[u, zp, 0], y2_recv.at[u, zp, 0], heads=up),
            remote(pp.at[u, zp, (y + 3) % 4], rb.at[u, zp], y2_send.at[u, zp, 1], y2_recv.at[u, zp, 1], heads=down),
        )

    far = 1 - zh

    def y_first(u):
        for zp in (far, zh):
            for copy in y1_copies(u, zp):
                copy.start()

    def y_second(u):
        for zp in (far, zh):
            for i, (first, second) in enumerate(zip(y1_copies(u, zp), y2_copies(u, zp))):
                first.wait_recv()
                yy = (y + 1 + 2 * i) % 4
                got = (yl, yr)[i]
                pp[u, zp, yy, i] = (pp[u, zp, yy, i].astype(F32) + got[u, zp].astype(F32)).astype(BF16)
                second.start()

    def z_copies(u, forward):
        out = []
        for i in range(2):
            to = (above, below)[i]
            if forward:
                out.append(remote(zr.at[u, i], rz.at[u, i], z2_send.at[u, i], z2_recv.at[u, i], ctx=zpart, heads=to))
            else:
                out.append(remote(zs.at[u, i], zr.at[u, i], z1_send.at[u, i], z1_recv.at[u, i], ctx=zpart, heads=to))
        return out

    def z_relay(u):
        for first, second in zip(z_copies(u, False), z_copies(u, True)):
            first.wait_recv()
            second.start()

    def y_total(u, zp):
        for copy in y2_copies(u, zp):
            copy.wait_recv()
        return pp[u, zp, y].astype(F32) + ra[u, zp].astype(F32) + rb[u, zp].astype(F32)

    def z_start(u):
        zs[u] = y_total(u, far).astype(BF16)
        for copy in z_copies(u, False):
            copy.start()

    def emit(u):
        total = y_total(u, zh)
        for copy in z_copies(u, True):
            copy.wait_recv()
        total = total + rz[u].astype(F32)
        for cc in range(2):
            rows = pl.ds(cc * hr * SUBS + u * hr, hr)
            out_ref[rows, :] = (res_ref[rows, :].astype(F32) + total[cc]).astype(BF16)

    load_k.wait()
    scores(0, 0, s_a, m_a)
    load_v.wait()
    scores(0, 1, s_b, m_b)
    mix(0, 0, s_a, m_a)
    pl.semaphore_wait(barrier, 1 + (CHIPS - 1) + 3)
    q_handle(0, 0)
    q_stage(1, 0)[0].start()
    mix(0, 1, s_b, m_b)
    q_wait_pair(0, 0)
    scores(1, 0, s_a, m_a)
    q_wait_pair(1, 0)
    scores(1, 1, s_b, m_b)
    mix(1, 0, s_a, m_a)
    for k in (1, 2, 3):
        q_handle(0, k)
    scores(2, 0, s_a, m_a)
    mix(1, 1, s_b, m_b)
    start_pair(0)

    events = {
        3: [lambda: q_handle(0, 4), lambda: q_handle(0, 6), lambda: q_handle(0, 7), lambda: q_rest(1)],
        5: [lambda: q_handle(0, 5), lambda: q_handle(1, 1), lambda: q_handle(1, 2), lambda: q_handle(1, 3)],
        7: [lambda: q_handle(1, 4), lambda: q_handle(1, 6), lambda: q_handle(1, 7)],
        9: [lambda: q_handle(1, 5), lambda: half_forward(0, 4)],
        10: [lambda: half_forward(0, 5)],
        12: [lambda: finish(0)],
        13: [lambda: half_forward(1, 4)],
        14: [lambda: a_handle(0, 1), lambda: a_handle(0, 2), lambda: a_handle(0, 3)],
        15: [lambda: half_forward(1, 5)],
    }

    def step(m, _):
        for parity in range(2):
            @pl.when(m % 2 == parity)
            def _():
                for at, acts in events.items():
                    if at % 2 == parity:
                        @pl.when(m == at)
                        def _():
                            for act in acts:
                                act()

        start_pair(m - 1)

        @pl.when(m >= SUBS + 2)
        def _():
            merge_pair(m - 2)
            far_pair = offset(sub_and_pair(m - 2)[1])[0] == 2

            @pl.when(jnp.logical_not(far_pair))
            def _():
                start_owner(m - 2)

            @pl.when(far_pair)
            def _():
                for u in range(SUBS):
                    for k in (4, 5):
                        @pl.when(m - 2 == step_of(u, k))
                        def _():
                            half_start(u, k)

        q_wait_pair(*sub_and_pair(m))
        nxt = jnp.minimum(m + 1, LAST)
        scores(m, 1, s_b, m_b)
        mix(m, 0, s_a, m_a)
        scores(nxt, 0, s_a, m_a)
        mix(m, 1, s_b, m_b)
        return 0

    lax.fori_loop(SUBS, LAST + 1, step, 0)

    early, late = (0, 1, 2, 3), (4, 6, 7, 5)

    def pairs_in(u, ks):
        for k in ks:
            a_wait_pair(u, k)

    start_pair(LAST)
    merge_pair(LAST - 1)
    start_owner(LAST - 1)
    load_w.wait()
    pairs_in(0, early)
    project(0, early)
    merge_pair(LAST)
    start_owner(LAST)
    a_handle(0, 4)
    a_handle(0, 6)
    a_handle(0, 7)
    q_drain(0)
    finish(1)
    a_handle(0, 5)
    q_drain(1)
    pairs_in(0, late)
    project(0, late)
    y_first(0)
    a_handle(1, 1)
    a_handle(1, 2)
    a_handle(1, 3)
    pairs_in(1, early)
    project(1, early)
    y_second(0)
    a_handle(1, 4)
    a_handle(1, 6)
    a_handle(1, 7)
    a_drain(0)
    a_handle(1, 5)
    pairs_in(1, late)
    project(1, late)
    y_first(1)
    z_start(0)

    def drain(m, _):
        for copy in pair_send(m):
            copy.wait_send()

        @pl.when((m >= SUBS) & (offset(sub_and_pair(m)[1])[0] != 2))
        def _():
            for copy in owner_send(m):
                copy.wait_send()

        return 0

    y_second(1)
    z_relay(0)
    lax.fori_loop(0, LAST + 1, drain, 0)
    z_start(1)
    emit(0)
    z_relay(1)
    a_drain(1)
    for u in range(SUBS):
        for k in (4, 5):
            for copy in half_copies(u, k, False) + half_copies(u, k, True):
                copy.wait_send()
    emit(1)

    for u in range(SUBS):
        for copy in z_copies(u, False) + z_copies(u, True):
            copy.wait_send()
        for zp in range(2):
            for copy in y1_copies(u, zp) + y2_copies(u, zp):
                copy.wait_send()


def shards(queries, cache_keys, cache_values, bounds, out_weight, residual):
    rows, cols = queries.shape
    prompts, span, hd = cache_keys.shape
    out_rows, width = residual.shape
    hr = rows // SUBS
    vmem = pl.BlockSpec(memory_space=pltpu.VMEM)
    hbm = pl.BlockSpec(memory_space=pl.ANY)
    n = SUBS * CHIPS
    unit = GROUPS * hr
    dma = lambda *s: pltpu.SemaphoreType.DMA(s)
    gather_sems = [
        dma(SUBS, 4), dma(SUBS, CHIPS), dma(SUBS, 8), dma(SUBS, CHIPS, 2), dma(SUBS, 4, 2),
    ]
    return pl.pallas_call(
        kernel,
        out_shape=jax.ShapeDtypeStruct(residual.shape, BF16),
        in_specs=[pl.BlockSpec(memory_space=pltpu.SMEM), vmem, hbm, hbm, hbm, vmem],
        out_specs=vmem,
        scratch_shapes=[
            pltpu.VMEM((SUBS, CHIPS, 2, hr, cols), BF16),
            pltpu.VMEM((prompts, span, hd), BF16),
            pltpu.VMEM((prompts, span, 2 * hd), BF16),
            pltpu.VMEM(out_weight.shape, BF16),
            pltpu.VMEM((unit, span), F32),
            pltpu.VMEM((unit, span), F32),
            pltpu.VMEM((unit, hd), F32),
            pltpu.VMEM((unit, hd), F32),
            pltpu.VMEM((n, 2, hr, cols), BF16),
            pltpu.VMEM((n, 2, hr, hd), F32),
            pltpu.VMEM((n, hr, cols), BF16),
            pltpu.VMEM((n, hr, hd), F32),
            pltpu.VMEM((n, hr, cols), BF16),
            pltpu.VMEM((n, hr, hd), F32),
            pltpu.VMEM((n, hr, cols), BF16),
            pltpu.VMEM((n, hr, hd), F32),
            pltpu.VMEM((2 * SUBS, hr, cols), BF16),
            pltpu.VMEM((2 * SUBS, hr, hd), F32),
            pltpu.VMEM((SUBS, CHIPS, 2, hr, cols), BF16),
            pltpu.VMEM((SUBS, 2, 4, 2, hr, width), BF16),
            pltpu.VMEM((SUBS, 2, hr, width), BF16),
            pltpu.VMEM((SUBS, 2, hr, width), BF16),
            pltpu.VMEM((SUBS, 2, 2, hr, width), BF16),
            pltpu.VMEM((SUBS, 2, 2, hr, width), BF16),
            pltpu.VMEM((SUBS, 2, hr, width), BF16),
            pltpu.VMEM((SUBS, 2, hr, width), BF16),
            pltpu.VMEM((SUBS, 2, hr, width), BF16),
            dma(3), *gather_sems, *gather_sems,
            dma(n), dma(n), dma(n), dma(n),
            dma(n), dma(n), dma(n), dma(n),
            dma(SUBS, 2, 2), dma(SUBS, 2, 2), dma(SUBS, 2, 2), dma(SUBS, 2, 2),
            dma(SUBS, 2), dma(SUBS, 2), dma(SUBS, 2), dma(SUBS, 2),
            dma(2 * SUBS, 2, 2), dma(2 * SUBS, 2, 2), dma(2 * SUBS, 2, 2), dma(2 * SUBS, 2, 2),
        ],
        compiler_params=pltpu.CompilerParams(
            collective_id=0, has_side_effects=True, vmem_limit_bytes=62 * 1024 * 1024
        ),
    )(bounds, queries, cache_keys, cache_values, out_weight, residual)


def solution(mesh):
    in_specs = (
        P("ctx", "heads"),
        P(None, "ctx", "heads"),
        P(None, "ctx", "heads"),
        P(),
        P("heads", "ctx"),
        P("heads", "ctx"),
    )
    out_specs = P("heads", "ctx")
    return jax.shard_map(shards, mesh=mesh, in_specs=in_specs, out_specs=out_specs, check_vma=False)
```

```python
import functools
import math

import jax
import jax.numpy as jnp
from jax import lax
from jax.experimental import pallas as pl
from jax.experimental.pallas import tpu as pltpu
from jax.sharding import PartitionSpec as P

H = 128
KV = 8
HD = 128
GROUPS = H // KV
NEG = -1e30
LOG2E = 1.4426950408889634
SCALE2 = LOG2E / math.sqrt(HD)
CHIPS = 8
SUBS = 2
LAST = SUBS * CHIPS - 1
BF16 = jnp.bfloat16
F32 = jnp.float32
MESH = pl.DeviceIdType.MESH
OFFSETS = ((0, 0), (0, 1), (1, 0), (3, 0), (2, 0), (2, 1), (1, 1), (3, 1))
STEPS = tuple(
    [(0, 0), (1, 0)]
    + [(0, k) for k in (1, 2, 6, 7, 5, 4, 3)]
    + [(1, k) for k in (5, 6, 7, 4, 1, 2, 3)]
)


def pick(k, values):
    if isinstance(k, int):
        return values[k]
    out = values[0]
    for j in range(1, len(values)):
        out = jnp.where(k == j, values[j], out)
    return out


def offset(k):
    return pick(k, [o[0] for o in OFFSETS]), pick(k, [o[1] for o in OFFSETS])


def sub_and_pair(m):
    return pick(m, [u for u, _ in STEPS]), pick(m, [k for _, k in STEPS])


def step_of(u, k):
    return STEPS.index((u, k))


def unit_of(m, i):
    if isinstance(m, int) and m < SUBS:
        return i, 0, m
    return *sub_and_pair(m), i


def slot_of(m, i):
    return (i, m) if isinstance(m, int) and m < SUBS else (m, i)


def kernel(
    bounds, q_ref, k_hbm, v_hbm, w_hbm, res_ref, out_hbm,
    q_all, k_buf, v_buf, w_buf, s_a, s_b, m_a, m_b,
    o_all, lse_all, rc, rc_lse, mx, mx_lse, rx, rx_lse, xr, xr_lse,
    mz, mz_lse, rm, rm_lse,
    att, pp, yl, yr, ra, rb, zs, zr, rz,
    out_ref, local_sem, out_sem, *sems,
):
    q_sems, a_sems, (c_send, c_recv, cl_send, cl_recv), (x_send, x_recv, xl_send, xl_recv), (
        y1_send, y1_recv, y2_send, y2_recv, z1_send, z1_recv, z2_send, z2_recv,
        h1_send, h1_recv, m_send, m_recv,
    ) = sems[:5], sems[5:10], sems[10:14], sems[14:18], sems[18:]
    me = lax.axis_index("ctx")
    hd = lax.axis_index("heads")
    x, zl, c = me // 4, (me // 2) % 2, me % 2
    zh, y = hd // 4, hd % 4
    hr = q_ref.shape[0] // SUBS
    hh = hr // 2
    span = k_buf.shape[1]
    unit = GROUPS * hr

    def ctx_at(dx, dz, dc):
        return ((x + dx) % 4) * 4 + ((zl + dz) % 2) * 2 + (c + dc) % 2

    partner = ctx_at(0, 0, 1)
    zpart = ctx_at(0, 1, 0)
    right = ctx_at(1, 0, 0)
    left = ctx_at(3, 0, 0)
    up = zh * 4 + (y + 1) % 4
    down = zh * 4 + (y + 3) % 4
    above = ((zh + zl) % 2) * 4 + y
    below = ((zh + 1 - zl) % 2) * 4 + y
    other = (1 - zh) * 4 + y

    def remote(src, dst, send, recv, **where):
        return pltpu.make_async_remote_copy(
            src_ref=src, dst_ref=dst, send_sem=send, recv_sem=recv,
            device_id=where, device_id_type=MESH,
        )

    load_k = pltpu.make_async_copy(k_hbm, k_buf, local_sem.at[0])
    load_v = pltpu.make_async_copy(v_hbm, v_buf.at[:, :, pl.ds(0, HD)], local_sem.at[1])
    load_w = pltpu.make_async_copy(w_hbm, w_buf, local_sem.at[2])
    load_k.start()
    load_v.start()
    load_w.start()

    barrier = pltpu.get_barrier_semaphore()
    pl.semaphore_signal(barrier, inc=1, device_id={"ctx": partner}, device_id_type=MESH)
    for k in range(1, CHIPS):
        dx, dz = offset(k)
        pl.semaphore_signal(barrier, inc=1, device_id={"ctx": ctx_at(dx, dz, 0)}, device_id_type=MESH)
    for to in (up, down):
        pl.semaphore_signal(barrier, inc=1, device_id={"heads": to}, device_id_type=MESH)
    pl.semaphore_signal(barrier, inc=1, device_id={"ctx": zpart, "heads": other}, device_id_type=MESH)
    for u in range(SUBS):
        q_all[u, 0, 0] = q_ref[pl.ds(u * hr, hr), :]
    for p in range(2):
        v_buf[p, :, pl.ds(HD, HD)] = jnp.ones((span, HD), BF16)

    def gather(buf, sems, own):
        s0, sc, sh, rv, rh = sems

        def whole(u, k, dc, send, to, src=None):
            return remote(buf.at[u, k, dc] if src is None else src, buf.at[u, k, dc], send, rv.at[u, k, dc], ctx=to)

        def part(u, k, top, src_k, send, to):
            i = 0 if top else 1
            rows = pl.ds(i * hh, hh)
            return remote(buf.at[u, src_k, 0, rows], buf.at[u, k, 0, rows], send, rh.at[u, k - 4, i], ctx=to)

        top, bottom = True, False

        def stage(u, k):
            if k == 0:
                src = own(u)
                return [
                    whole(u, 1, 0, s0.at[u, 1], zpart, src),
                    whole(u, 3, 0, s0.at[u, 2], right, src),
                    whole(u, 2, 0, s0.at[u, 3], left, src),
                    whole(u, 0, 1, s0.at[u, 0], partner, src),
                ]
            here = buf.at[u, k, 0]
            out = []
            if k == 1:
                out.append(part(u, 7, bottom, 1, sh.at[u, 4], right))
                out.append(part(u, 6, bottom, 1, sh.at[u, 5], left))
            if k == 2:
                out.append(part(u, 6, top, 2, sh.at[u, 6], zpart))
                out.append(part(u, 4, bottom, 2, sh.at[u, 0], left))
            if k == 3:
                out.append(part(u, 7, top, 3, sh.at[u, 7], zpart))
                out.append(part(u, 4, top, 3, sh.at[u, 1], right))
            if k == 6:
                out.append(part(u, 5, bottom, 6, sh.at[u, 2], left))
            if k == 7:
                out.append(part(u, 5, top, 7, sh.at[u, 3], right))
            out.append(whole(u, k, 1, sc.at[u, k], partner, here))
            return out

        def arrive(u, k):
            if k >= 4:
                part(u, k, True, k, sh.at[u, 0], right).wait_recv()
                part(u, k, False, k, sh.at[u, 0], left).wait_recv()
            else:
                whole(u, k, 0, s0.at[u, 0], partner).wait_recv()

        def handle(u, k):
            links(u, k)
            core(u, k)

        def links(u, k):
            if k:
                arrive(u, k)
            for copy in stage(u, k)[:-1]:
                copy.start()

        def core(u, k):
            stage(u, k)[-1].start()

        def wait_pair(u, k):
            whole(u, k, 1, s0.at[0, 0], partner).wait_recv()

        def drain(u):
            for k in range(CHIPS):
                for copy in stage(u, k):
                    copy.wait_send()

        return handle, wait_pair, drain, links, core

    q_handle, q_wait_pair, q_drain, q_rest, q_core = gather(q_all, q_sems, lambda u: q_ref.at[pl.ds(u * hr, hr)])
    a_handle, a_wait_pair, a_drain, a_links, a_core = gather(att, a_sems, lambda u: att.at[u, 0, 0])

    def place(u, k, dc):
        dx, dz = offset(k)
        t = ctx_at(dx, dz, dc)
        return t // 8, (t % 8) * (hr * SUBS) + u * hr

    def scores(m, i, s_ref, m_ref):
        u, k, dc = unit_of(m, i)
        p, within = place(u, k, dc)
        block = jnp.concatenate(
            [q_all[u, k, dc, :, pl.ds(j * HD, HD)] for j in range(GROUPS)], axis=0
        )
        s = lax.dot_general(
            block, k_buf[p], (((1,), (1,)), ((), ())), preferred_element_type=F32
        )
        row = lax.broadcasted_iota(jnp.int32, (hr, 1), 0)
        limit = jnp.minimum(bounds[p, 0] + within + row, bounds[p, 1] - 1) - me * span
        limit = jnp.concatenate([limit] * GROUPS, axis=0)
        key = lax.broadcasted_iota(jnp.int32, (unit, span), 1)
        s = jnp.where(key <= limit, s, NEG)
        s_ref[...] = s
        m_ref[...] = jnp.broadcast_to(jnp.max(s, axis=1, keepdims=True), (unit, HD))

    def mix(m, i, s_ref, m_ref):
        u, k, dc = unit_of(m, i)
        p, _ = place(u, k, dc)
        to, core = slot_of(m, i)
        top = m_ref[...]
        weights = jnp.exp2((s_ref[...] - jnp.concatenate([top] * (span // HD), axis=1)) * SCALE2)
        both = jnp.dot(weights.astype(BF16), v_buf[p], preferred_element_type=F32)
        total = both[:, HD:]
        mixed = (both[:, :HD] / total).astype(BF16)
        lane = lax.broadcasted_iota(jnp.int32, (hr, HD), 1)
        m_c = jnp.zeros((hr, HD), F32)
        t_c = jnp.ones((hr, HD), F32)
        for h in range(GROUPS):
            part = slice(h * hr, (h + 1) * hr)
            o_all[to, core, :, pl.ds(h * HD, HD)] = mixed[part]
            m_c = jnp.where(lane == h, top[part], m_c)
            t_c = jnp.where(lane == h, total[part], t_c)
        lse_all[to, core] = m_c * SCALE2 + jnp.log(t_c) * LOG2E

    def merge(parts, out, out_lse):
        lses = [lse[...] for _, lse in parts]
        count = lses[0].shape[0]
        top = functools.reduce(jnp.maximum, lses)
        es = [jnp.exp2(lse - top) for lse in lses]
        tot = functools.reduce(lambda a, b: a + b, es)
        inv = 1.0 / tot
        if out_lse is not None:
            out_lse[...] = top + jnp.log(tot) * LOG2E
        ws = [e * inv for e in es]
        for h in range(GROUPS):
            cols = pl.ds(h * HD, HD)
            acc = None
            for (o, _), w in zip(parts, ws):
                term = o[:, cols].astype(F32) * jnp.broadcast_to(w[:, h:h + 1], (count, HD))
                acc = term if acc is None else acc + term
            out[:, cols] = acc.astype(BF16)

    def pair_send(m):
        return (
            remote(o_all.at[m, 1], rc.at[m], c_send.at[m], c_recv.at[m], ctx=partner),
            remote(lse_all.at[m, 1], rc_lse.at[m], cl_send.at[m], cl_recv.at[m], ctx=partner),
        )

    def owner_send(m):
        _, k = sub_and_pair(m)
        dx, _ = offset(k)
        to = ctx_at(dx, 0, 0)
        return (
            remote(mx.at[m], rx.at[m], x_send.at[m], x_recv.at[m], ctx=to),
            remote(mx_lse.at[m], rx_lse.at[m], xl_send.at[m], xl_recv.at[m], ctx=to),
        )

    def half_copies(u, k):
        m, d = step_of(u, k), 2 * u + k - 4
        out = []
        for i in range(2):
            rows, to = pl.ds(i * hh, hh), (right, left)[i]
            out.append(remote(mx.at[m, rows], xr.at[d, rows], h1_send.at[d, i, 0], h1_recv.at[d, i, 0], ctx=to))
            out.append(remote(mx_lse.at[m, rows], xr_lse.at[d, rows], h1_send.at[d, i, 1], h1_recv.at[d, i, 1], ctx=to))
        return out

    def half_start(u, k):
        for copy in half_copies(u, k):
            copy.start()

    def absorb(u, k):
        m, i, via = step_of(u, k), k % 2, 4 + k // 6
        d = 2 * u + via - 4
        rows = pl.ds(i * hh, hh)
        for copy in half_copies(u, via)[2 * i:2 * i + 2]:
            copy.wait_recv()
        merge(
            [(mx.at[m, rows], mx_lse.at[m, rows]), (xr.at[d, rows], xr_lse.at[d, rows])],
            mx.at[m, rows], mx_lse.at[m, rows],
        )
        start_owner(m)

    def start_pair(m):
        for copy in pair_send(m):
            copy.start()

    def merge_pair(m):
        for copy in pair_send(m):
            copy.wait_recv()
        merge_local(m)

    def merge_local(m):
        merge(
            [(o_all.at[m, 0], lse_all.at[m, 0]), (rc.at[m], rc_lse.at[m])],
            mx.at[m], mx_lse.at[m],
        )

    def start_owner(m):
        for copy in owner_send(m):
            copy.start()

    def received(u, k):
        for copy in owner_send(step_of(u, k)):
            copy.wait_recv()
        m = step_of(u, k)
        return rx.at[m], rx_lse.at[m]

    def row_copies(u):
        return (
            remote(mz.at[u], rm.at[u], m_send.at[u, 0], m_recv.at[u, 0], ctx=zpart),
            remote(mz_lse.at[u], rm_lse.at[u], m_send.at[u, 1], m_recv.at[u, 1], ctx=zpart),
        )

    def row_merge(u):
        own = step_of(u, 1)
        parts = [(mx.at[own], mx_lse.at[own])] + [received(u, k) for k in (6, 7)]
        merge(parts, mz.at[u], mz_lse.at[u])
        for copy in row_copies(u):
            copy.start()

    def finish(u):
        for copy in pair_send(u):
            copy.wait_recv()
        parts = [(o_all.at[u, 0], lse_all.at[u, 0]), (rc.at[u], rc_lse.at[u])]
        parts += [received(u, k) for k in (2, 3)]
        for copy in row_copies(u):
            copy.wait_recv()
        merge(parts + [(rm.at[u], rm_lse.at[u])], att.at[u, 0, 0], None)
        a_handle(u, 0)

    def project(u, ks):
        block = jnp.concatenate([att[u, k, dc] for k in ks for dc in range(2)], axis=0)
        done = jnp.dot(block, w_buf[...], preferred_element_type=F32).astype(BF16)
        i = 0
        for k in ks:
            dx, dz = offset(k)
            hp = ((x + dx) % 4) * 2 + (zl + dz) % 2
            for dc in range(2):
                pp[u, hp // 4, hp % 4, (c + dc) % 2] = done[i * hr:(i + 1) * hr]
                i += 1

    def y1_copies(u, zp):
        yy = (y + 2) % 4
        return (
            remote(pp.at[u, zp, yy, 0], yl.at[u, zp], y1_send.at[u, zp, 0], y1_recv.at[u, zp, 0], heads=up),
            remote(pp.at[u, zp, yy, 1], yr.at[u, zp], y1_send.at[u, zp, 1], y1_recv.at[u, zp, 1], heads=down),
        )

    def y2_copies(u, zp):
        return (
            remote(pp.at[u, zp, (y + 1) % 4], ra.at[u, zp], y2_send.at[u, zp, 0], y2_recv.at[u, zp, 0], heads=up),
            remote(pp.at[u, zp, (y + 3) % 4], rb.at[u, zp], y2_send.at[u, zp, 1], y2_recv.at[u, zp, 1], heads=down),
        )

    far = 1 - zh

    def y_first(u):
        for zp in (far, zh):
            for copy in y1_copies(u, zp):
                copy.start()

    def y_second(u):
        for zp in (far, zh):
            for i, (first, second) in enumerate(zip(y1_copies(u, zp), y2_copies(u, zp))):
                first.wait_recv()
                yy = (y + 1 + 2 * i) % 4
                got = (yl, yr)[i]
                pp[u, zp, yy, i] = (pp[u, zp, yy, i].astype(F32) + got[u, zp].astype(F32)).astype(BF16)
                second.start()

    def z_copies(u, forward):
        out = []
        for i in range(2):
            to = (above, below)[i]
            if forward:
                out.append(remote(zr.at[u, i], rz.at[u, i], z2_send.at[u, i], z2_recv.at[u, i], ctx=zpart, heads=to))
            else:
                out.append(remote(zs.at[u, i], zr.at[u, i], z1_send.at[u, i], z1_recv.at[u, i], ctx=zpart, heads=to))
        return out

    def z_relay(u):
        for first, second in zip(z_copies(u, False), z_copies(u, True)):
            first.wait_recv()
            second.start()

    def y_total(u, zp):
        for copy in y2_copies(u, zp):
            copy.wait_recv()
        return pp[u, zp, y].astype(F32) + ra[u, zp].astype(F32) + rb[u, zp].astype(F32)

    def z_start(u):
        zs[u] = y_total(u, far).astype(BF16)
        for copy in z_copies(u, False):
            copy.start()

    def emit(u):
        total = y_total(u, zh)
        for copy in z_copies(u, True):
            copy.wait_recv()
        total = total + rz[u].astype(F32)
        for cc in range(2):
            rows = pl.ds(cc * hr * SUBS + u * hr, hr)
            out_ref[rows, :] = (res_ref[rows, :].astype(F32) + total[cc]).astype(BF16)
            out_copy(u, cc).start()

    def out_copy(u, cc):
        rows = pl.ds(cc * hr * SUBS + u * hr, hr)
        return pltpu.make_async_copy(out_ref.at[rows], out_hbm.at[rows], out_sem.at[u, cc])

    load_k.wait()
    scores(0, 0, s_a, m_a)
    load_v.wait()
    scores(0, 1, s_b, m_b)
    mix(0, 0, s_a, m_a)
    o_all[LAST + 1, 0] = jnp.zeros((hr, GROUPS * HD), BF16)
    rc[LAST + 1] = jnp.zeros((hr, GROUPS * HD), BF16)
    lse_all[LAST + 1, 0] = jnp.zeros((hr, HD), F32)
    rc_lse[LAST + 1] = jnp.zeros((hr, HD), F32)
    pl.semaphore_wait(barrier, 1 + (CHIPS - 1) + 3)
    q_core(0, 0)
    q_rest(0, 0)
    q_core(1, 0)
    mix(0, 1, s_b, m_b)
    q_wait_pair(0, 0)
    scores(1, 0, s_a, m_a)
    q_wait_pair(1, 0)
    scores(1, 1, s_b, m_b)
    mix(1, 0, s_a, m_a)
    for k in (1, 2, 3):
        q_handle(0, k)
    scores(2, 0, s_a, m_a)
    mix(1, 1, s_b, m_b)
    start_pair(0)

    events = {
        2: [lambda: q_rest(1, 0)],
        3: [lambda: q_handle(0, 6), lambda: q_handle(0, 7), lambda: q_handle(0, 4)],
        4: [lambda: q_handle(1, 1), lambda: q_handle(1, 2), lambda: q_handle(1, 3)],
        5: [lambda: q_handle(0, 5)],
        6: [lambda: q_handle(1, 6), lambda: q_handle(1, 7), lambda: q_handle(1, 4)],
        8: [lambda: q_handle(1, 5)],
        9: [lambda: half_start(0, 5)],
        10: [lambda: half_start(0, 4)],
        11: [lambda: absorb(0, 6), lambda: absorb(0, 7)],
        12: [lambda: half_start(1, 5), lambda: absorb(0, 2), lambda: absorb(0, 3)],
        13: [lambda: row_merge(0)],
        14: [lambda: absorb(1, 6), lambda: absorb(1, 7)],
        15: [lambda: half_start(1, 4), lambda: finish(0)],
    }

    def step(m, _):
        for parity in range(2):
            @pl.when(m % 2 == parity)
            def _():
                for at, acts in events.items():
                    if at % 2 == parity:
                        @pl.when(m == at)
                        def _():
                            for act in acts:
                                act()

        start_pair(m - 1)

        @pl.when(m >= SUBS + 2)
        def _():
            for copy in pair_send(m - 2):
                copy.wait_recv()

        q_wait_pair(*sub_and_pair(m))
        nxt = jnp.minimum(m + 1, LAST)
        scores(m, 1, s_b, m_b)
        mix(m, 0, s_a, m_a)
        scores(nxt, 0, s_a, m_a)
        mix(m, 1, s_b, m_b)
        merge_local(jnp.where(m >= SUBS + 2, m - 2, LAST + 1))
        return 0

    lax.fori_loop(SUBS, LAST + 1, step, 0)

    early, late = (0, 1, 2, 3), (4, 6, 7, 5)

    def pairs_in(u, ks):
        for k in ks:
            a_wait_pair(u, k)

    start_pair(LAST)
    merge_pair(LAST - 1)
    row_merge(1)
    absorb(1, 2)
    merge_pair(LAST)
    absorb(1, 3)
    for k in (1, 2, 3):
        a_links(0, k)
    for k in (1, 2, 3):
        a_core(0, k)
    load_w.wait()
    q_drain(0)
    q_drain(1)
    finish(1)
    for k in (6, 7, 4):
        a_handle(0, k)
    pairs_in(0, early)
    project(0, early)
    for k in (1, 2, 3):
        a_handle(1, k)
    a_handle(0, 5)
    pairs_in(0, late)
    project(0, late)
    y_first(0)
    pairs_in(1, early)
    project(1, early)
    for k in (6, 7, 4):
        a_handle(1, k)
    y_second(0)
    a_handle(1, 5)
    a_drain(0)
    pairs_in(1, late)
    project(1, late)
    y_first(1)
    z_start(0)

    def drain(m, _):
        for copy in pair_send(m):
            copy.wait_send()

        @pl.when((m >= SUBS) & (offset(sub_and_pair(m)[1])[0] % 2 == 1))
        def _():
            for copy in owner_send(m):
                copy.wait_send()

        return 0

    y_second(1)
    z_relay(0)
    lax.fori_loop(0, LAST + 1, drain, 0)
    z_start(1)
    emit(0)
    z_relay(1)
    a_drain(1)
    for u in range(SUBS):
        for k in (4, 5):
            for copy in half_copies(u, k):
                copy.wait_send()
        for copy in row_copies(u):
            copy.wait_send()
    emit(1)

    for u in range(SUBS):
        for cc in range(2):
            out_copy(u, cc).wait()
        for copy in z_copies(u, False) + z_copies(u, True):
            copy.wait_send()
        for zp in range(2):
            for copy in y1_copies(u, zp) + y2_copies(u, zp):
                copy.wait_send()


def shards(queries, cache_keys, cache_values, bounds, out_weight, residual):
    rows, cols = queries.shape
    prompts, span, hd = cache_keys.shape
    out_rows, width = residual.shape
    hr = rows // SUBS
    vmem = pl.BlockSpec(memory_space=pltpu.VMEM)
    hbm = pl.BlockSpec(memory_space=pl.ANY)
    n = SUBS * CHIPS
    unit = GROUPS * hr
    dma = lambda *s: pltpu.SemaphoreType.DMA(s)
    gather_sems = [
        dma(SUBS, 4), dma(SUBS, CHIPS), dma(SUBS, 8), dma(SUBS, CHIPS, 2), dma(SUBS, 4, 2),
    ]
    return pl.pallas_call(
        kernel,
        out_shape=jax.ShapeDtypeStruct(residual.shape, BF16),
        in_specs=[pl.BlockSpec(memory_space=pltpu.SMEM), vmem, hbm, hbm, hbm, vmem],
        out_specs=hbm,
        scratch_shapes=[
            pltpu.VMEM((SUBS, CHIPS, 2, hr, cols), BF16),
            pltpu.VMEM((prompts, span, hd), BF16),
            pltpu.VMEM((prompts, span, 2 * hd), BF16),
            pltpu.VMEM(out_weight.shape, BF16),
            pltpu.VMEM((unit, span), F32),
            pltpu.VMEM((unit, span), F32),
            pltpu.VMEM((unit, hd), F32),
            pltpu.VMEM((unit, hd), F32),
            pltpu.VMEM((n + 1, 2, hr, cols), BF16),
            pltpu.VMEM((n + 1, 2, hr, hd), F32),
            pltpu.VMEM((n + 1, hr, cols), BF16),
            pltpu.VMEM((n + 1, hr, hd), F32),
            pltpu.VMEM((n + 1, hr, cols), BF16),
            pltpu.VMEM((n + 1, hr, hd), F32),
            pltpu.VMEM((n, hr, cols), BF16),
            pltpu.VMEM((n, hr, hd), F32),
            pltpu.VMEM((2 * SUBS, hr, cols), BF16),
            pltpu.VMEM((2 * SUBS, hr, hd), F32),
            pltpu.VMEM((SUBS, hr, cols), BF16),
            pltpu.VMEM((SUBS, hr, hd), F32),
            pltpu.VMEM((SUBS, hr, cols), BF16),
            pltpu.VMEM((SUBS, hr, hd), F32),
            pltpu.VMEM((SUBS, CHIPS, 2, hr, cols), BF16),
            pltpu.VMEM((SUBS, 2, 4, 2, hr, width), BF16),
            pltpu.VMEM((SUBS, 2, hr, width), BF16),
            pltpu.VMEM((SUBS, 2, hr, width), BF16),
            pltpu.VMEM((SUBS, 2, 2, hr, width), BF16),
            pltpu.VMEM((SUBS, 2, 2, hr, width), BF16),
            pltpu.VMEM((SUBS, 2, hr, width), BF16),
            pltpu.VMEM((SUBS, 2, hr, width), BF16),
            pltpu.VMEM((SUBS, 2, hr, width), BF16),
            pltpu.VMEM((out_rows, width), BF16),
            dma(3), dma(SUBS, 2), *gather_sems, *gather_sems,
            dma(n), dma(n), dma(n), dma(n),
            dma(n), dma(n), dma(n), dma(n),
            dma(SUBS, 2, 2), dma(SUBS, 2, 2), dma(SUBS, 2, 2), dma(SUBS, 2, 2),
            dma(SUBS, 2), dma(SUBS, 2), dma(SUBS, 2), dma(SUBS, 2),
            dma(2 * SUBS, 2, 2), dma(2 * SUBS, 2, 2),
            dma(SUBS, 2), dma(SUBS, 2),
        ],
        compiler_params=pltpu.CompilerParams(
            collective_id=0, has_side_effects=True, vmem_limit_bytes=62 * 1024 * 1024
        ),
    )(bounds, queries, cache_keys, cache_values, out_weight, residual)


def solution(mesh):
    in_specs = (
        P("ctx", "heads"),
        P(None, "ctx", "heads"),
        P(None, "ctx", "heads"),
        P(),
        P("heads", "ctx"),
        P("heads", "ctx"),
    )
    out_specs = P("heads", "ctx")
    return jax.shard_map(shards, mesh=mesh, in_specs=in_specs, out_specs=out_specs, check_vma=False)
```

```python
import functools
import math

import jax
import jax.numpy as jnp
from jax import lax
from jax.experimental import pallas as pl
from jax.experimental.pallas import tpu as pltpu
from jax.sharding import PartitionSpec as P

H = 128
KV = 8
HD = 128
GROUPS = H // KV
NEG = -1e30
LOG2E = 1.4426950408889634
SCALE2 = LOG2E / math.sqrt(HD)
CHIPS = 8
SUBS = 2
LAST = SUBS * CHIPS - 1
BF16 = jnp.bfloat16
F32 = jnp.float32
MESH = pl.DeviceIdType.MESH
OFFSETS = ((0, 0), (0, 1), (1, 0), (3, 0), (2, 0), (2, 1), (1, 1), (3, 1))
STEPS = tuple(
    [(0, 0), (1, 0)]
    + [(0, k) for k in (1, 2, 6, 7, 5, 4, 3)]
    + [(1, k) for k in (5, 6, 7, 4, 1, 2, 3)]
)


def pick(k, values):
    if isinstance(k, int):
        return values[k]
    out = values[0]
    for j in range(1, len(values)):
        out = jnp.where(k == j, values[j], out)
    return out


def offset(k):
    return pick(k, [o[0] for o in OFFSETS]), pick(k, [o[1] for o in OFFSETS])


def sub_and_pair(m):
    return pick(m, [u for u, _ in STEPS]), pick(m, [k for _, k in STEPS])


def step_of(u, k):
    return STEPS.index((u, k))


def unit_of(m, i):
    if isinstance(m, int) and m < SUBS:
        return i, 0, m
    return *sub_and_pair(m), i


def slot_of(m, i):
    return (i, m) if isinstance(m, int) and m < SUBS else (m, i)


def kernel(
    bounds, q_ref, k_hbm, v_hbm, w_hbm, res_ref, out_hbm,
    q_all, k_buf, v_buf, w_buf, s_a, s_b, m_a, m_b,
    o_all, lse_all, rc, rc_lse, mx, mx_lse, rx, rx_lse, xr, xr_lse,
    mz, mz_lse, rm, rm_lse,
    att, pp, yl, yr, ra, rb, zs, zr, rz,
    out_ref, local_sem, out_sem, *sems,
):
    q_sems, a_sems, (c_send, c_recv, cl_send, cl_recv), (x_send, x_recv, xl_send, xl_recv), (
        y1_send, y1_recv, y2_send, y2_recv, z1_send, z1_recv, z2_send, z2_recv,
        h1_send, h1_recv, m_send, m_recv,
    ) = sems[:5], sems[5:10], sems[10:14], sems[14:18], sems[18:]
    me = lax.axis_index("ctx")
    hd = lax.axis_index("heads")
    x, zl, c = me // 4, (me // 2) % 2, me % 2
    zh, y = hd // 4, hd % 4
    hr = q_ref.shape[0] // SUBS
    hh = hr // 2
    span = k_buf.shape[1]
    unit = GROUPS * hr

    def ctx_at(dx, dz, dc):
        return ((x + dx) % 4) * 4 + ((zl + dz) % 2) * 2 + (c + dc) % 2

    partner = ctx_at(0, 0, 1)
    zpart = ctx_at(0, 1, 0)
    right = ctx_at(1, 0, 0)
    left = ctx_at(3, 0, 0)
    up = zh * 4 + (y + 1) % 4
    down = zh * 4 + (y + 3) % 4
    above = ((zh + zl) % 2) * 4 + y
    below = ((zh + 1 - zl) % 2) * 4 + y
    other = (1 - zh) * 4 + y

    def remote(src, dst, send, recv, **where):
        return pltpu.make_async_remote_copy(
            src_ref=src, dst_ref=dst, send_sem=send, recv_sem=recv,
            device_id=where, device_id_type=MESH,
        )

    load_k = pltpu.make_async_copy(k_hbm, k_buf, local_sem.at[0])
    load_v = pltpu.make_async_copy(v_hbm, v_buf.at[:, :, pl.ds(0, HD)], local_sem.at[1])
    load_w = pltpu.make_async_copy(w_hbm, w_buf, local_sem.at[2])
    load_k.start()
    load_v.start()
    load_w.start()

    barrier = pltpu.get_barrier_semaphore()
    pl.semaphore_signal(barrier, inc=1, device_id={"ctx": partner}, device_id_type=MESH)
    for k in range(1, CHIPS):
        dx, dz = offset(k)
        pl.semaphore_signal(barrier, inc=1, device_id={"ctx": ctx_at(dx, dz, 0)}, device_id_type=MESH)
    for to in (up, down):
        pl.semaphore_signal(barrier, inc=1, device_id={"heads": to}, device_id_type=MESH)
    pl.semaphore_signal(barrier, inc=1, device_id={"ctx": zpart, "heads": other}, device_id_type=MESH)
    for u in range(SUBS):
        q_all[u, 0, 0] = q_ref[pl.ds(u * hr, hr), :]
    for p in range(2):
        v_buf[p, :, pl.ds(HD, HD)] = jnp.ones((span, HD), BF16)

    def gather(buf, sems, own):
        s0, sc, sh, rv, rh = sems

        def whole(u, k, dc, send, to, src=None):
            return remote(buf.at[u, k, dc] if src is None else src, buf.at[u, k, dc], send, rv.at[u, k, dc], ctx=to)

        def part(u, k, top, src_k, send, to):
            i = 0 if top else 1
            rows = pl.ds(i * hh, hh)
            return remote(buf.at[u, src_k, 0, rows], buf.at[u, k, 0, rows], send, rh.at[u, k - 4, i], ctx=to)

        top, bottom = True, False

        def stage(u, k):
            if k == 0:
                src = own(u)
                return [
                    whole(u, 1, 0, s0.at[u, 1], zpart, src),
                    whole(u, 3, 0, s0.at[u, 2], right, src),
                    whole(u, 2, 0, s0.at[u, 3], left, src),
                    whole(u, 0, 1, s0.at[u, 0], partner, src),
                ]
            here = buf.at[u, k, 0]
            out = []
            if k == 1:
                out.append(part(u, 7, bottom, 1, sh.at[u, 4], right))
                out.append(part(u, 6, bottom, 1, sh.at[u, 5], left))
            if k == 2:
                out.append(part(u, 6, top, 2, sh.at[u, 6], zpart))
                out.append(part(u, 4, bottom, 2, sh.at[u, 0], left))
            if k == 3:
                out.append(part(u, 7, top, 3, sh.at[u, 7], zpart))
                out.append(part(u, 4, top, 3, sh.at[u, 1], right))
            if k == 6:
                out.append(part(u, 5, bottom, 6, sh.at[u, 2], left))
            if k == 7:
                out.append(part(u, 5, top, 7, sh.at[u, 3], right))
            out.append(whole(u, k, 1, sc.at[u, k], partner, here))
            return out

        def arrive(u, k):
            if k >= 4:
                part(u, k, True, k, sh.at[u, 0], right).wait_recv()
                part(u, k, False, k, sh.at[u, 0], left).wait_recv()
            else:
                whole(u, k, 0, s0.at[u, 0], partner).wait_recv()

        def handle(u, k):
            links(u, k)
            core(u, k)

        def links(u, k):
            if k:
                arrive(u, k)
            for copy in stage(u, k)[:-1]:
                copy.start()

        def core(u, k):
            stage(u, k)[-1].start()

        def wait_pair(u, k):
            whole(u, k, 1, s0.at[0, 0], partner).wait_recv()

        def drain(u):
            for k in range(CHIPS):
                for copy in stage(u, k):
                    copy.wait_send()

        return handle, wait_pair, drain, links, core

    q_handle, q_wait_pair, q_drain, q_rest, q_core = gather(q_all, q_sems, lambda u: q_ref.at[pl.ds(u * hr, hr)])
    a_handle, a_wait_pair, a_drain, a_links, a_core = gather(att, a_sems, lambda u: att.at[u, 0, 0])

    def place(u, k, dc):
        dx, dz = offset(k)
        t = ctx_at(dx, dz, dc)
        return t // 8, (t % 8) * (hr * SUBS) + u * hr

    def scores(m, i, s_ref, m_ref):
        u, k, dc = unit_of(m, i)
        p, within = place(u, k, dc)
        block = jnp.concatenate(
            [q_all[u, k, dc, :, pl.ds(j * HD, HD)] for j in range(GROUPS)], axis=0
        )
        s = lax.dot_general(
            block, k_buf[p], (((1,), (1,)), ((), ())), preferred_element_type=F32
        )
        row = lax.broadcasted_iota(jnp.int32, (hr, 1), 0)
        limit = jnp.minimum(bounds[p, 0] + within + row, bounds[p, 1] - 1) - me * span
        limit = jnp.concatenate([limit] * GROUPS, axis=0)
        key = lax.broadcasted_iota(jnp.int32, (unit, span), 1)
        s = jnp.where(key <= limit, s, NEG)
        s_ref[...] = s
        m_ref[...] = jnp.broadcast_to(jnp.max(s, axis=1, keepdims=True), (unit, HD))

    def mix(m, i, s_ref, m_ref):
        u, k, dc = unit_of(m, i)
        p, _ = place(u, k, dc)
        to, core = slot_of(m, i)
        top = m_ref[...]
        weights = jnp.exp2((s_ref[...] - jnp.concatenate([top] * (span // HD), axis=1)) * SCALE2)
        both = jnp.dot(weights.astype(BF16), v_buf[p], preferred_element_type=F32)
        total = both[:, HD:]
        mixed = (both[:, :HD] / total).astype(BF16)
        lane = lax.broadcasted_iota(jnp.int32, (hr, HD), 1)
        m_c = jnp.zeros((hr, HD), F32)
        t_c = jnp.ones((hr, HD), F32)
        for h in range(GROUPS):
            part = slice(h * hr, (h + 1) * hr)
            o_all[to, core, :, pl.ds(h * HD, HD)] = mixed[part]
            m_c = jnp.where(lane == h, top[part], m_c)
            t_c = jnp.where(lane == h, total[part], t_c)
        lse_all[to, core] = m_c * SCALE2 + jnp.log(t_c) * LOG2E

    def merge(parts, out, out_lse):
        lses = [lse[...] for _, lse in parts]
        count = lses[0].shape[0]
        top = functools.reduce(jnp.maximum, lses)
        es = [jnp.exp2(lse - top) for lse in lses]
        tot = functools.reduce(lambda a, b: a + b, es)
        inv = 1.0 / tot
        if out_lse is not None:
            out_lse[...] = top + jnp.log(tot) * LOG2E
        ws = [e * inv for e in es]
        for h in range(GROUPS):
            cols = pl.ds(h * HD, HD)
            acc = None
            for (o, _), w in zip(parts, ws):
                term = o[:, cols].astype(F32) * jnp.broadcast_to(w[:, h:h + 1], (count, HD))
                acc = term if acc is None else acc + term
            out[:, cols] = acc.astype(BF16)

    def pair_send(m):
        return (
            remote(o_all.at[m, 1], rc.at[m], c_send.at[m], c_recv.at[m], ctx=partner),
            remote(lse_all.at[m, 1], rc_lse.at[m], cl_send.at[m], cl_recv.at[m], ctx=partner),
        )

    def owner_send(m):
        _, k = sub_and_pair(m)
        dx, _ = offset(k)
        to = ctx_at(dx, 0, 0)
        return (
            remote(mx.at[m], rx.at[m], x_send.at[m], x_recv.at[m], ctx=to),
            remote(mx_lse.at[m], rx_lse.at[m], xl_send.at[m], xl_recv.at[m], ctx=to),
        )

    def half_copies(u, k):
        m, d = step_of(u, k), 2 * u + k - 4
        out = []
        for i in range(2):
            rows, to = pl.ds(i * hh, hh), (right, left)[i]
            out.append(remote(mx.at[m, rows], xr.at[d, rows], h1_send.at[d, i, 0], h1_recv.at[d, i, 0], ctx=to))
            out.append(remote(mx_lse.at[m, rows], xr_lse.at[d, rows], h1_send.at[d, i, 1], h1_recv.at[d, i, 1], ctx=to))
        return out

    def half_start(u, k):
        for copy in half_copies(u, k):
            copy.start()

    def absorb(u, k):
        m, i, via = step_of(u, k), k % 2, 4 + k // 6
        d = 2 * u + via - 4
        rows = pl.ds(i * hh, hh)
        for copy in half_copies(u, via)[2 * i:2 * i + 2]:
            copy.wait_recv()
        merge(
            [(mx.at[m, rows], mx_lse.at[m, rows]), (xr.at[d, rows], xr_lse.at[d, rows])],
            mx.at[m, rows], mx_lse.at[m, rows],
        )
        start_owner(m)

    def start_pair(m):
        for copy in pair_send(m):
            copy.start()

    def merge_pair(m):
        for copy in pair_send(m):
            copy.wait_recv()
        merge_local(m)

    def merge_local(m):
        merge(
            [(o_all.at[m, 0], lse_all.at[m, 0]), (rc.at[m], rc_lse.at[m])],
            mx.at[m], mx_lse.at[m],
        )

    def start_owner(m):
        for copy in owner_send(m):
            copy.start()

    def received(u, k):
        for copy in owner_send(step_of(u, k)):
            copy.wait_recv()
        m = step_of(u, k)
        return rx.at[m], rx_lse.at[m]

    def row_copies(u):
        return (
            remote(mz.at[u], rm.at[u], m_send.at[u, 0], m_recv.at[u, 0], ctx=zpart),
            remote(mz_lse.at[u], rm_lse.at[u], m_send.at[u, 1], m_recv.at[u, 1], ctx=zpart),
        )

    def row_merge(u):
        own = step_of(u, 1)
        parts = [(mx.at[own], mx_lse.at[own])] + [received(u, k) for k in (6, 7)]
        merge(parts, mz.at[u], mz_lse.at[u])
        for copy in row_copies(u):
            copy.start()

    def finish(u):
        for copy in pair_send(u):
            copy.wait_recv()
        parts = [(o_all.at[u, 0], lse_all.at[u, 0]), (rc.at[u], rc_lse.at[u])]
        parts += [received(u, k) for k in (2, 3)]
        for copy in row_copies(u):
            copy.wait_recv()
        merge(parts + [(rm.at[u], rm_lse.at[u])], att.at[u, 0, 0], None)
        a_handle(u, 0)

    def project(u, ks):
        block = jnp.concatenate([att[u, k, dc] for k in ks for dc in range(2)], axis=0)
        done = jnp.dot(block, w_buf[...], preferred_element_type=F32).astype(BF16)
        i = 0
        for k in ks:
            dx, dz = offset(k)
            hp = ((x + dx) % 4) * 2 + (zl + dz) % 2
            for dc in range(2):
                pp[u, hp // 4, hp % 4, (c + dc) % 2] = done[i * hr:(i + 1) * hr]
                i += 1

    def y1_copies(u, zp):
        yy = (y + 2) % 4
        return (
            remote(pp.at[u, zp, yy, 0], yl.at[u, zp], y1_send.at[u, zp, 0], y1_recv.at[u, zp, 0], heads=up),
            remote(pp.at[u, zp, yy, 1], yr.at[u, zp], y1_send.at[u, zp, 1], y1_recv.at[u, zp, 1], heads=down),
        )

    def y2_copies(u, zp):
        return (
            remote(pp.at[u, zp, (y + 1) % 4], ra.at[u, zp], y2_send.at[u, zp, 0], y2_recv.at[u, zp, 0], heads=up),
            remote(pp.at[u, zp, (y + 3) % 4], rb.at[u, zp], y2_send.at[u, zp, 1], y2_recv.at[u, zp, 1], heads=down),
        )

    far = 1 - zh

    def y_first(u):
        for zp in (far, zh):
            for copy in y1_copies(u, zp):
                copy.start()

    def y_second(u):
        for zp in (far, zh):
            for i, (first, second) in enumerate(zip(y1_copies(u, zp), y2_copies(u, zp))):
                first.wait_recv()
                yy = (y + 1 + 2 * i) % 4
                got = (yl, yr)[i]
                pp[u, zp, yy, i] = (pp[u, zp, yy, i].astype(F32) + got[u, zp].astype(F32)).astype(BF16)
                second.start()

    def z_copies(u, forward):
        out = []
        for i in range(2):
            to = (above, below)[i]
            if forward:
                out.append(remote(zr.at[u, i], rz.at[u, i], z2_send.at[u, i], z2_recv.at[u, i], ctx=zpart, heads=to))
            else:
                out.append(remote(zs.at[u, i], zr.at[u, i], z1_send.at[u, i], z1_recv.at[u, i], ctx=zpart, heads=to))
        return out

    def z_relay(u):
        for first, second in zip(z_copies(u, False), z_copies(u, True)):
            first.wait_recv()
            second.start()

    def y_total(u, zp):
        for copy in y2_copies(u, zp):
            copy.wait_recv()
        return pp[u, zp, y].astype(F32) + ra[u, zp].astype(F32) + rb[u, zp].astype(F32)

    def z_start(u):
        zs[u] = y_total(u, far).astype(BF16)
        for copy in z_copies(u, False):
            copy.start()

    def emit(u):
        total = y_total(u, zh)
        for copy in z_copies(u, True):
            copy.wait_recv()
        total = total + rz[u].astype(F32)
        for cc in range(2):
            rows = pl.ds(cc * hr * SUBS + u * hr, hr)
            out_ref[rows, :] = (res_ref[rows, :].astype(F32) + total[cc]).astype(BF16)
            out_copy(u, cc).start()

    def out_copy(u, cc):
        rows = pl.ds(cc * hr * SUBS + u * hr, hr)
        return pltpu.make_async_copy(out_ref.at[rows], out_hbm.at[rows], out_sem.at[u, cc])

    load_k.wait()
    scores(0, 0, s_a, m_a)
    load_v.wait()
    scores(0, 1, s_b, m_b)
    mix(0, 0, s_a, m_a)
    o_all[LAST + 1, 0] = jnp.zeros((hr, GROUPS * HD), BF16)
    rc[LAST + 1] = jnp.zeros((hr, GROUPS * HD), BF16)
    lse_all[LAST + 1, 0] = jnp.zeros((hr, HD), F32)
    rc_lse[LAST + 1] = jnp.zeros((hr, HD), F32)
    pl.semaphore_wait(barrier, 1 + (CHIPS - 1) + 3)
    q_core(0, 0)
    q_rest(0, 0)
    q_core(1, 0)
    mix(0, 1, s_b, m_b)
    q_wait_pair(0, 0)
    scores(1, 0, s_a, m_a)
    q_wait_pair(1, 0)
    scores(1, 1, s_b, m_b)
    mix(1, 0, s_a, m_a)
    for k in (1, 2, 3):
        q_handle(0, k)
    scores(2, 0, s_a, m_a)
    mix(1, 1, s_b, m_b)
    start_pair(0)

    events = {
        2: [lambda: q_rest(1, 0)],
        3: [lambda: q_handle(0, 6), lambda: q_handle(0, 7), lambda: q_handle(0, 4)],
        4: [lambda: q_handle(1, 1), lambda: q_handle(1, 2), lambda: q_handle(1, 3)],
        5: [lambda: q_handle(0, 5)],
        6: [lambda: q_handle(1, 6), lambda: q_handle(1, 7), lambda: q_handle(1, 4)],
        8: [lambda: q_handle(1, 5)],
        9: [lambda: half_start(0, 5)],
        10: [lambda: half_start(0, 4), lambda: absorb(0, 6), lambda: absorb(0, 7)],
        12: [lambda: half_start(1, 5), lambda: absorb(0, 2), lambda: absorb(0, 3), lambda: row_merge(0)],
        14: [lambda: absorb(1, 6), lambda: absorb(1, 7), lambda: finish(0)],
        15: [lambda: half_start(1, 4)],
    }

    def step(m, _):
        for parity in range(2):
            @pl.when(m % 2 == parity)
            def _():
                for at, acts in events.items():
                    if at % 2 == parity:
                        @pl.when(m == at)
                        def _():
                            for act in acts:
                                act()

        start_pair(m - 1)

        @pl.when(m >= SUBS + 2)
        def _():
            for copy in pair_send(m - 2):
                copy.wait_recv()

        q_wait_pair(*sub_and_pair(m))
        nxt = jnp.minimum(m + 1, LAST)
        scores(m, 1, s_b, m_b)
        mix(m, 0, s_a, m_a)
        scores(nxt, 0, s_a, m_a)
        mix(m, 1, s_b, m_b)
        merge_local(jnp.where(m >= SUBS + 2, m - 2, LAST + 1))
        return 0

    lax.fori_loop(SUBS, LAST + 1, step, 0)

    early, late = (0, 1, 2, 3), (4, 6, 7, 5)

    def pairs_in(u, ks):
        for k in ks:
            a_wait_pair(u, k)

    start_pair(LAST)
    for k in (1, 2, 3):
        a_links(0, k)
    merge_pair(LAST - 1)
    row_merge(1)
    absorb(1, 2)
    merge_pair(LAST)
    absorb(1, 3)
    for k in (1, 2, 3):
        a_core(0, k)
    load_w.wait()
    q_drain(0)
    pairs_in(0, early)
    project(0, early)
    finish(1)
    for k in (6, 7, 4):
        a_handle(0, k)
    q_drain(1)
    a_handle(0, 5)
    pairs_in(0, late)
    project(0, late)
    y_first(0)
    for k in (1, 2, 3):
        a_handle(1, k)
    y_second(0)
    pairs_in(1, early)
    project(1, early)
    for k in (6, 7, 4):
        a_handle(1, k)
    a_drain(0)
    a_handle(1, 5)
    z_start(0)
    pairs_in(1, late)
    project(1, late)
    y_first(1)
    z_relay(0)
    emit(0)

    def drain(m, _):
        for copy in pair_send(m):
            copy.wait_send()

        @pl.when((m >= SUBS) & (offset(sub_and_pair(m)[1])[0] % 2 == 1))
        def _():
            for copy in owner_send(m):
                copy.wait_send()

        return 0

    y_second(1)
    lax.fori_loop(0, LAST + 1, drain, 0)
    z_start(1)
    z_relay(1)
    a_drain(1)
    for u in range(SUBS):
        for k in (4, 5):
            for copy in half_copies(u, k):
                copy.wait_send()
        for copy in row_copies(u):
            copy.wait_send()
    emit(1)

    for u in range(SUBS):
        for cc in range(2):
            out_copy(u, cc).wait()
        for copy in z_copies(u, False) + z_copies(u, True):
            copy.wait_send()
        for zp in range(2):
            for copy in y1_copies(u, zp) + y2_copies(u, zp):
                copy.wait_send()


def shards(queries, cache_keys, cache_values, bounds, out_weight, residual):
    rows, cols = queries.shape
    prompts, span, hd = cache_keys.shape
    out_rows, width = residual.shape
    hr = rows // SUBS
    vmem = pl.BlockSpec(memory_space=pltpu.VMEM)
    hbm = pl.BlockSpec(memory_space=pl.ANY)
    n = SUBS * CHIPS
    unit = GROUPS * hr
    dma = lambda *s: pltpu.SemaphoreType.DMA(s)
    gather_sems = [
        dma(SUBS, 4), dma(SUBS, CHIPS), dma(SUBS, 8), dma(SUBS, CHIPS, 2), dma(SUBS, 4, 2),
    ]
    return pl.pallas_call(
        kernel,
        out_shape=jax.ShapeDtypeStruct(residual.shape, BF16),
        in_specs=[pl.BlockSpec(memory_space=pltpu.SMEM), vmem, hbm, hbm, hbm, vmem],
        out_specs=hbm,
        scratch_shapes=[
            pltpu.VMEM((SUBS, CHIPS, 2, hr, cols), BF16),
            pltpu.VMEM((prompts, span, hd), BF16),
            pltpu.VMEM((prompts, span, 2 * hd), BF16),
            pltpu.VMEM(out_weight.shape, BF16),
            pltpu.VMEM((unit, span), F32),
            pltpu.VMEM((unit, span), F32),
            pltpu.VMEM((unit, hd), F32),
            pltpu.VMEM((unit, hd), F32),
            pltpu.VMEM((n + 1, 2, hr, cols), BF16),
            pltpu.VMEM((n + 1, 2, hr, hd), F32),
            pltpu.VMEM((n + 1, hr, cols), BF16),
            pltpu.VMEM((n + 1, hr, hd), F32),
            pltpu.VMEM((n + 1, hr, cols), BF16),
            pltpu.VMEM((n + 1, hr, hd), F32),
            pltpu.VMEM((n, hr, cols), BF16),
            pltpu.VMEM((n, hr, hd), F32),
            pltpu.VMEM((2 * SUBS, hr, cols), BF16),
            pltpu.VMEM((2 * SUBS, hr, hd), F32),
            pltpu.VMEM((SUBS, hr, cols), BF16),
            pltpu.VMEM((SUBS, hr, hd), F32),
            pltpu.VMEM((SUBS, hr, cols), BF16),
            pltpu.VMEM((SUBS, hr, hd), F32),
            pltpu.VMEM((SUBS, CHIPS, 2, hr, cols), BF16),
            pltpu.VMEM((SUBS, 2, 4, 2, hr, width), BF16),
            pltpu.VMEM((SUBS, 2, hr, width), BF16),
            pltpu.VMEM((SUBS, 2, hr, width), BF16),
            pltpu.VMEM((SUBS, 2, 2, hr, width), BF16),
            pltpu.VMEM((SUBS, 2, 2, hr, width), BF16),
            pltpu.VMEM((SUBS, 2, hr, width), BF16),
            pltpu.VMEM((SUBS, 2, hr, width), BF16),
            pltpu.VMEM((SUBS, 2, hr, width), BF16),
            pltpu.VMEM((out_rows, width), BF16),
            dma(3), dma(SUBS, 2), *gather_sems, *gather_sems,
            dma(n), dma(n), dma(n), dma(n),
            dma(n), dma(n), dma(n), dma(n),
            dma(SUBS, 2, 2), dma(SUBS, 2, 2), dma(SUBS, 2, 2), dma(SUBS, 2, 2),
            dma(SUBS, 2), dma(SUBS, 2), dma(SUBS, 2), dma(SUBS, 2),
            dma(2 * SUBS, 2, 2), dma(2 * SUBS, 2, 2),
            dma(SUBS, 2), dma(SUBS, 2),
        ],
        compiler_params=pltpu.CompilerParams(
            collective_id=0, has_side_effects=True, vmem_limit_bytes=62 * 1024 * 1024
        ),
    )(bounds, queries, cache_keys, cache_values, out_weight, residual)


def solution(mesh):
    in_specs = (
        P("ctx", "heads"),
        P(None, "ctx", "heads"),
        P(None, "ctx", "heads"),
        P(),
        P("heads", "ctx"),
        P("heads", "ctx"),
    )
    out_specs = P("heads", "ctx")
    return jax.shard_map(shards, mesh=mesh, in_specs=in_specs, out_specs=out_specs, check_vma=False)
```
